32 devices in a mesh: ctx: 8 (over y, x, core), fsdp: 4 (over z).
Axes of the slice: x: 2, y: 2, z: 4, core: 2. Of those that a mesh axis runs over, the one named last changes fastest.
Arguments:
- hidden_in: bfloat16 [4096, 2048], P(('ctx', 'fsdp')), may hold values from -16 to 16
- pair_order: int32 [8], replicated, may hold values from 0 to 7, each once
- attn_gain: bfloat16 [2048], P(('ctx', 'fsdp')), may hold values from 0.099609375 to 1.8984375
- w_query: bfloat16 [2048, 2048], P(('ctx', 'fsdp')), may hold values from -0.21875 to 0.21875
- key_weight_matrix: bfloat16 [2048, 512], P(('ctx', 'fsdp')), may hold values from -0.21875 to 0.21875
- value_weight_matrix: bfloat16 [2048, 512], P(('ctx', 'fsdp')), may hold values from -0.125 to 0.125
- w_out: bfloat16 [2048, 2048], P(('ctx', 'fsdp')), may hold values from -0.125 to 0.125
- mlp_gain: bfloat16 [2048], P(('ctx', 'fsdp')), may hold values from 0.099609375 to 1.8984375
- w_gate: bfloat16 [2048, 8192], P(('ctx', 'fsdp')), may hold values from -0.125 to 0.125
- w_up: bfloat16 [2048, 8192], P(('ctx', 'fsdp')), may hold values from -0.125 to 0.125
- w_down: bfloat16 [8192, 2048], P(None, ('ctx', 'fsdp')), may hold values from -0.0625 to 0.0625
- out_grad: bfloat16 [4096, 2048], P(('ctx', 'fsdp')), may hold values from -6 to 6
Outputs:
- result: float32 [4096, 2048], P(('ctx', 'fsdp'))
- grad_in: float32 [4096, 2048], P(('ctx', 'fsdp'))
- grad_attn_gain: float32 [2048], P(('ctx', 'fsdp'))
- grad_query: float32 [2048, 2048], P(('ctx', 'fsdp'))
- grad_key: float32 [2048, 512], P(('ctx', 'fsdp'))
- grad_value: float32 [2048, 512], P(('ctx', 'fsdp'))
- grad_out: float32 [2048, 2048], P(('ctx', 'fsdp'))
- grad_mlp_gain: float32 [2048], P(('ctx', 'fsdp'))
- grad_gate: float32 [2048, 8192], P(('ctx', 'fsdp'))
- grad_up: float32 [2048, 8192], P(('ctx', 'fsdp'))
- grad_down: float32 [8192, 2048], P(None, ('ctx', 'fsdp'))
The draws below stay inside these ranges and needn't reach their ends.
Inputs may be any that keep to these rules, and one draw needn't show every extreme that they name: `pair_order`: a permutation of the 8 pairs of causal blocks.
All inputs are finite; a program needn't handle non-finite values.
Results may differ from the reference program's by a relative error of at most 0.017.
The reference program's roundings to bfloat16 on the way count: a program that leaves them out, or rounds other values in their place, can miss the bound.
Values may be sent and summed in bfloat16 or wider, within the bound.
No kernel may reach another device: no remote copies, remote signals or barrier semaphores. Data moves between devices by JAX's collectives and lax.ppermute only.
A program may use at most 512 MiB of HBM per device.

```python
import jax
import jax.numpy as jnp
from jax import lax

MODEL_WIDTH = 2048
QUERY_HEADS = 32
KEY_VALUE_HEADS = 8
HEAD_SIZE = 64
FF = 8192
TOK_DEV = 128
TOKEN_COUNT = 4096
PAIRS = 8
HALF = 64
SPAN = 256
GROUP_ROWS = 512
QUERY_GROUP = 4


def draw_hidden_in(key, part):
    base_key, column_key, row_key = jax.random.split(key, 3)
    base_draw = jax.random.normal(base_key, (TOKEN_COUNT, MODEL_WIDTH), jnp.float32)
    column_scale = jnp.exp(jax.random.uniform(column_key, (1, MODEL_WIDTH), jnp.float32, -1.15, 1.15))
    row_scale = jnp.exp(jax.random.uniform(row_key, (TOKEN_COUNT, 1), jnp.float32, -0.7, 0.7))
    values = row_scale * base_draw * column_scale
    return jnp.clip(values, -16.0, 16.0).astype(jnp.bfloat16)


def shard_levels(key, dims, shards, least, high):
    def one(axis_at, blocks):
        heights = jax.random.uniform(jax.random.fold_in(jax.random.fold_in(key, 6), axis_at), (blocks,), jnp.float32, least / len(shards), high / len(shards))
        return jnp.repeat(jnp.exp(heights), dims[axis_at] // blocks).reshape((-1,) + (1,) * (len(dims) - axis_at - 1))

    gain = one(*shards[0])
    for cut in shards[1:]:
        gain = gain * one(*cut)
    return gain


def scatter_about(stream_key, extent, deviation, bound, pieces=(), kind=jnp.bfloat16):
    array = deviation * jax.random.normal(stream_key, extent, jnp.float32)
    if pieces:
        array = array * shard_levels(stream_key, extent, pieces, -0.22, 0.18)
    return jnp.clip(array, -bound, bound).astype(kind)


def setup_inputs(seed: int = 0) -> dict:
    key_list = jax.random.split(jax.random.key(seed), 13)
    hidden_in = draw_hidden_in(jax.random.fold_in(key_list[12], 71), 0)
    pair_order = jax.random.permutation(key_list[1], PAIRS).astype(jnp.int32)
    attn_gain = jnp.clip(1.0 + 0.18 * jax.random.normal(key_list[2], (MODEL_WIDTH,), jnp.float32), 0.099609375, 1.8984375).astype(jnp.bfloat16)
    w_query = scatter_about(key_list[3], (MODEL_WIDTH, QUERY_HEADS * HEAD_SIZE), (MODEL_WIDTH // 3) ** -0.5, 0.21875, ((0, 32),))
    key_weight_matrix = scatter_about(key_list[4], (MODEL_WIDTH, KEY_VALUE_HEADS * HEAD_SIZE), (MODEL_WIDTH // 3) ** -0.5, 0.21875, ((0, 32),))
    value_weight_matrix = scatter_about(key_list[5], (MODEL_WIDTH, KEY_VALUE_HEADS * HEAD_SIZE), MODEL_WIDTH ** -0.5, 0.125, ((0, 32),))
    w_out = scatter_about(key_list[6], (QUERY_HEADS * HEAD_SIZE, MODEL_WIDTH), (QUERY_HEADS * HEAD_SIZE) ** -0.5, 0.125, ((0, 32),))
    mlp_gain = jnp.clip(1.0 + 0.18 * jax.random.normal(key_list[7], (MODEL_WIDTH,), jnp.float32), 0.099609375, 1.8984375).astype(jnp.bfloat16)
    w_gate = scatter_about(key_list[8], (MODEL_WIDTH, FF), MODEL_WIDTH ** -0.5, 0.125, ((0, 32),))
    w_up = scatter_about(key_list[9], (MODEL_WIDTH, FF), MODEL_WIDTH ** -0.5, 0.125, ((0, 32),))
    w_down = scatter_about(key_list[10], (FF, MODEL_WIDTH), FF ** -0.5, 0.0625, ((1, 32),))
    out_grad = scatter_about(key_list[11], (TOKEN_COUNT, MODEL_WIDTH), 1.0, 6.0, ((0, 32),))
    return dict(hidden_in=hidden_in, pair_order=pair_order, attn_gain=attn_gain, w_query=w_query, key_weight_matrix=key_weight_matrix, value_weight_matrix=value_weight_matrix, w_out=w_out, mlp_gain=mlp_gain, w_gate=w_gate, w_up=w_up, w_down=w_down, out_grad=out_grad)


rope_base = 500000.0
norm_eps = 1e-05

def token_positions(pair_order):
    row_index = jnp.arange(TOKEN_COUNT, dtype=jnp.int32)
    owner_group = row_index // GROUP_ROWS
    inner_row = row_index % GROUP_ROWS
    shard_index = inner_row // TOK_DEV
    local_row = inner_row % TOK_DEV
    pair_block = jnp.take(pair_order, owner_group)
    block_number = jnp.where(local_row < HALF, pair_block, 2 * PAIRS - 1 - pair_block)
    return (block_number * SPAN + shard_index * HALF + local_row % HALF).astype(jnp.int32)

def rope_tables(positions):
    frequency = 1.0 / rope_base ** (jnp.arange(0, HEAD_SIZE, 2, dtype=jnp.float32) / HEAD_SIZE)
    angles = positions.astype(jnp.float32)[:, None] * frequency[None, :]
    return (jnp.cos(angles)[:, None, :], jnp.sin(angles)[:, None, :])

def apply_rotation(values, cosine_factor, sine_lookup):
    first_half = values[..., :HEAD_SIZE // 2]
    second_half = values[..., HEAD_SIZE // 2:]
    return jnp.concatenate([first_half * cosine_factor - second_half * sine_lookup, second_half * cosine_factor + first_half * sine_lookup], axis=-1)

def attention_forward(heads_q, heads_k, heads_v, positions):
    block_rows = min(4096, TOKEN_COUNT)
    score_scale = HEAD_SIZE ** (-0.5)

    def one_head(operands):
        q_head, k_head, v_head = operands

        def block_step(carried, block_index):
            q_rows = lax.dynamic_slice_in_dim(q_head, block_index * block_rows, block_rows, 0)
            q_pos = lax.dynamic_slice_in_dim(positions, block_index * block_rows, block_rows, 0)
            scores = jnp.dot(q_rows, k_head.T, preferred_element_type=jnp.float32) * score_scale
            weights = jnp.where(positions[None, :] <= q_pos[:, None], jnp.exp(scores), 0.0)
            totals = lax.optimization_barrier(jnp.sum(weights, axis=1))
            head_out = jnp.dot(weights.astype(jnp.bfloat16), v_head, preferred_element_type=jnp.float32) / totals[:, None]
            return (carried, (head_out, totals))
        unused, (head_out, totals) = lax.scan(block_step, 0, jnp.arange(TOKEN_COUNT // block_rows, dtype=jnp.int32))
        return (head_out.reshape(TOKEN_COUNT, HEAD_SIZE), totals.reshape(TOKEN_COUNT))
    return lax.map(one_head, (heads_q, heads_k, heads_v))

def attention_backward(heads_q, heads_k, heads_v, positions, out_heads, totals, grad_heads):
    block_rows = min(4096, TOKEN_COUNT)
    score_scale = HEAD_SIZE ** (-0.5)

    def one_head(operands):
        q_head, k_head, v_head, o_head, t_head, g_head = operands
        delta_rows = lax.optimization_barrier(jnp.sum(g_head.astype(jnp.float32) * o_head, axis=1))

        def block_step(carried, block_index):
            d_keys, d_values = carried
            row_start = block_index * block_rows
            q_rows = lax.dynamic_slice_in_dim(q_head, row_start, block_rows, 0)
            q_pos = lax.dynamic_slice_in_dim(positions, row_start, block_rows, 0)
            t_rows = lax.dynamic_slice_in_dim(t_head, row_start, block_rows, 0)
            g_rows = lax.dynamic_slice_in_dim(g_head, row_start, block_rows, 0)
            delta_part = lax.dynamic_slice_in_dim(delta_rows, row_start, block_rows, 0)
            scores = jnp.dot(q_rows, k_head.T, preferred_element_type=jnp.float32) * score_scale
            probabilities = jnp.where(positions[None, :] <= q_pos[:, None], jnp.exp(scores) / t_rows[:, None], 0.0)
            prob_grads = jnp.dot(g_rows, v_head.T, preferred_element_type=jnp.float32)
            score_grads = (probabilities * (prob_grads - delta_part[:, None]) * score_scale).astype(jnp.bfloat16)
            d_query = jnp.dot(score_grads, k_head, preferred_element_type=jnp.float32)
            d_keys = d_keys + jnp.dot(score_grads.T, q_rows, preferred_element_type=jnp.float32)
            d_values = d_values + jnp.dot(probabilities.astype(jnp.bfloat16).T, g_rows, preferred_element_type=jnp.float32)
            return ((d_keys, d_values), d_query)
        zero_rows = jnp.zeros((TOKEN_COUNT, HEAD_SIZE), jnp.float32)
        (d_keys, d_values), d_query = lax.scan(block_step, (zero_rows, zero_rows), jnp.arange(TOKEN_COUNT // block_rows, dtype=jnp.int32))
        return (d_query.reshape(TOKEN_COUNT, HEAD_SIZE), d_keys, d_values)
    return lax.map(one_head, (heads_q, heads_k, heads_v, out_heads, totals, grad_heads))

def reference(hidden_in, pair_order, attn_gain, w_query, key_weight_matrix, value_weight_matrix, w_out, mlp_gain, w_gate, w_up, w_down, out_grad):
    positions = token_positions(pair_order)
    cosine_factor, sine_lookup = rope_tables(positions)
    residual = hidden_in.astype(jnp.float32)
    scale_one = lax.rsqrt(lax.optimization_barrier(jnp.mean(residual * residual, axis=1, keepdims=True)) + norm_eps)
    unit_one = residual * scale_one
    first_normed_input = (unit_one * attn_gain.astype(jnp.float32)).astype(jnp.bfloat16)
    query_raw = jnp.dot(first_normed_input, w_query, preferred_element_type=jnp.float32).reshape(TOKEN_COUNT, QUERY_HEADS, HEAD_SIZE)
    key_unrotated = jnp.dot(first_normed_input, key_weight_matrix, preferred_element_type=jnp.float32).reshape(TOKEN_COUNT, KEY_VALUE_HEADS, HEAD_SIZE)
    value_projected = jnp.dot(first_normed_input, value_weight_matrix, preferred_element_type=jnp.float32).reshape(TOKEN_COUNT, KEY_VALUE_HEADS, HEAD_SIZE)
    query_rot = apply_rotation(query_raw, cosine_factor, sine_lookup).astype(jnp.bfloat16)
    key_rot = apply_rotation(key_unrotated, cosine_factor, sine_lookup).astype(jnp.bfloat16)
    value_bf = value_projected.astype(jnp.bfloat16)
    heads_q = query_rot.transpose(1, 0, 2)
    heads_k = jnp.repeat(key_rot.transpose(1, 0, 2), QUERY_GROUP, axis=0)
    heads_v = jnp.repeat(value_bf.transpose(1, 0, 2), QUERY_GROUP, axis=0)
    out_heads, totals = attention_forward(heads_q, heads_k, heads_v, positions)
    attn_bf = out_heads.transpose(1, 0, 2).reshape(TOKEN_COUNT, QUERY_HEADS * HEAD_SIZE).astype(jnp.bfloat16)
    after_attn = residual + jnp.dot(attn_bf, w_out, preferred_element_type=jnp.float32)
    block_rows = min(4096, TOKEN_COUNT)
    gain_two = mlp_gain.astype(jnp.float32)

    def ffn_block(carried, block_index):
        grad_gate_sum, grad_up_sum, grad_down_sum, gain_sum = carried
        row_start = block_index * block_rows
        h_rows = lax.dynamic_slice_in_dim(after_attn, row_start, block_rows, 0)
        grad_rows = lax.dynamic_slice_in_dim(out_grad, row_start, block_rows, 0)
        scale_two = lax.rsqrt(lax.optimization_barrier(jnp.mean(h_rows * h_rows, axis=1, keepdims=True)) + norm_eps)
        unit_two = h_rows * scale_two
        normed_two = (unit_two * gain_two).astype(jnp.bfloat16)
        gate_proj = jnp.dot(normed_two, w_gate, preferred_element_type=jnp.float32)
        up_proj = jnp.dot(normed_two, w_up, preferred_element_type=jnp.float32)
        sigmoid_gate = jax.nn.sigmoid(gate_proj)
        activated = (gate_proj * sigmoid_gate * up_proj).astype(jnp.bfloat16)
        block_result = h_rows + jnp.dot(activated, w_down, preferred_element_type=jnp.float32)
        d_act = jnp.dot(grad_rows, w_down.T, preferred_element_type=jnp.float32)
        d_gate = (d_act * up_proj * sigmoid_gate * (1.0 + gate_proj * (1.0 - sigmoid_gate))).astype(jnp.bfloat16)
        d_up = (d_act * gate_proj * sigmoid_gate).astype(jnp.bfloat16)
        grad_down_sum = grad_down_sum + jnp.dot(activated.T, grad_rows, preferred_element_type=jnp.float32)
        grad_gate_sum = grad_gate_sum + jnp.dot(normed_two.T, d_gate, preferred_element_type=jnp.float32)
        grad_up_sum = grad_up_sum + jnp.dot(normed_two.T, d_up, preferred_element_type=jnp.float32)
        d_normed = jnp.dot(d_gate, w_gate.T, preferred_element_type=jnp.float32) + jnp.dot(d_up, w_up.T, preferred_element_type=jnp.float32)
        gain_sum = gain_sum + lax.optimization_barrier(jnp.sum(d_normed * unit_two, axis=0))
        d_unit = d_normed * gain_two
        d_mixed = grad_rows.astype(jnp.float32) + scale_two * (d_unit - unit_two * lax.optimization_barrier(jnp.mean(d_unit * unit_two, axis=1, keepdims=True)))
        return ((grad_gate_sum, grad_up_sum, grad_down_sum, gain_sum), (block_result, d_mixed))
    initial = (jnp.zeros((MODEL_WIDTH, FF), jnp.float32), jnp.zeros((MODEL_WIDTH, FF), jnp.float32), jnp.zeros((FF, MODEL_WIDTH), jnp.float32), jnp.zeros((MODEL_WIDTH,), jnp.float32))
    (grad_gate, grad_up, grad_down, grad_mlp_gain), (result, d_mixed) = lax.scan(ffn_block, initial, jnp.arange(TOKEN_COUNT // block_rows, dtype=jnp.int32))
    result = result.reshape(TOKEN_COUNT, MODEL_WIDTH)
    d_mixed = d_mixed.reshape(TOKEN_COUNT, MODEL_WIDTH)
    d_attn_bf = d_mixed.astype(jnp.bfloat16)
    grad_out = jnp.dot(attn_bf.T, d_attn_bf, preferred_element_type=jnp.float32)
    d_attn_out = jnp.dot(d_attn_bf, w_out.T, preferred_element_type=jnp.float32).astype(jnp.bfloat16)
    grad_heads = d_attn_out.reshape(TOKEN_COUNT, QUERY_HEADS, HEAD_SIZE).transpose(1, 0, 2)
    d_q_heads, key_head_gradient, value_head_gradient = attention_backward(heads_q, heads_k, heads_v, positions, out_heads, totals, grad_heads)
    d_query = d_q_heads.transpose(1, 0, 2)
    key_gradient = lax.optimization_barrier(jnp.sum(key_head_gradient.reshape(KEY_VALUE_HEADS, QUERY_GROUP, TOKEN_COUNT, HEAD_SIZE), axis=1)).transpose(1, 0, 2)
    value_gradient = lax.optimization_barrier(jnp.sum(value_head_gradient.reshape(KEY_VALUE_HEADS, QUERY_GROUP, TOKEN_COUNT, HEAD_SIZE), axis=1)).transpose(1, 0, 2)
    query_pre_grad = apply_rotation(d_query, cosine_factor, -sine_lookup).reshape(TOKEN_COUNT, QUERY_HEADS * HEAD_SIZE).astype(jnp.bfloat16)
    key_prerotation_gradient = apply_rotation(key_gradient, cosine_factor, -sine_lookup).reshape(TOKEN_COUNT, KEY_VALUE_HEADS * HEAD_SIZE).astype(jnp.bfloat16)
    value_gradient_bfloat = value_gradient.reshape(TOKEN_COUNT, KEY_VALUE_HEADS * HEAD_SIZE).astype(jnp.bfloat16)
    grad_query = jnp.dot(first_normed_input.T, query_pre_grad, preferred_element_type=jnp.float32)
    grad_key = jnp.dot(first_normed_input.T, key_prerotation_gradient, preferred_element_type=jnp.float32)
    grad_value = jnp.dot(first_normed_input.T, value_gradient_bfloat, preferred_element_type=jnp.float32)
    d_normed_one = jnp.dot(query_pre_grad, w_query.T, preferred_element_type=jnp.float32)
    d_normed_one = d_normed_one + jnp.dot(key_prerotation_gradient, key_weight_matrix.T, preferred_element_type=jnp.float32)
    d_normed_one = d_normed_one + jnp.dot(value_gradient_bfloat, value_weight_matrix.T, preferred_element_type=jnp.float32)
    grad_attn_gain = lax.optimization_barrier(jnp.sum(d_normed_one * unit_one, axis=0))
    d_unit_one = d_normed_one * attn_gain.astype(jnp.float32)
    grad_in = d_mixed + scale_one * (d_unit_one - unit_one * lax.optimization_barrier(jnp.mean(d_unit_one * unit_one, axis=1, keepdims=True)))
    return (result, grad_in, grad_attn_gain, grad_query, grad_key, grad_value, grad_out, grad_mlp_gain, grad_gate, grad_up, grad_down)
```

```python
import functools

import jax
import jax.numpy as jnp
from jax import lax
from jax.experimental import pallas as pl
from jax.experimental.pallas import tpu as pltpu
from jax.sharding import PartitionSpec as P

QUERY_HEADS = 32
KEY_VALUE_HEADS = 8
HEAD_SIZE = 64
LANES = 128

rope_base = 500000.0
norm_eps = 1e-05
BOTH = ("ctx", "fsdp")
BF16, F32 = jnp.bfloat16, jnp.float32


NT = (((1,), (1,)), ((), ()))
TN = (((0,), (0,)), ((), ()))
NN = (((1,), (0,)), ((), ()))


def mm(a, b, dims=NN, out=F32):
    return lax.dot_general(a, b, dims, preferred_element_type=F32).astype(out)


def shift_perm(n, s):
    return [(i, (i + s) % n) for i in range(n)]


def z_gather(x):
    n = lax.axis_size("fsdp")
    parts = [x] + [lax.ppermute(x, "fsdp", shift_perm(n, s)) for s in range(1, n)]
    return jnp.concatenate(parts, axis=0)


def z_reduce(partial):
    n = lax.axis_size("fsdp")
    rows = partial.shape[0] // n
    total = partial[:rows].astype(F32)
    for s in range(1, n):
        piece = partial[s * rows : (s + 1) * rows].astype(BF16)
        total = total + lax.ppermute(piece, "fsdp", shift_perm(n, -s)).astype(F32)
    return total


def z_exchange(pick):
    n, me = lax.axis_size("fsdp"), lax.axis_index("fsdp")
    own = pick(me)
    out = jnp.zeros((n,) + own.shape, own.dtype)
    out = lax.dynamic_update_index_in_dim(out, own, me, 0)
    for s in range(1, n):
        got = lax.ppermute(pick((me + s) % n), "fsdp", shift_perm(n, s))
        out = lax.dynamic_update_index_in_dim(out, got, (me - s) % n, 0)
    return out


def ctx_gather(x):
    return lax.all_gather(x, "ctx", axis=0, tiled=True)


def ctx_reduce(x):
    return lax.psum_scatter(x, "ctx", scatter_dimension=0, tiled=True)


def rotate_tile(x, cosine, sine):
    lane = lax.broadcasted_iota(jnp.int32, x.shape, 1)
    low = (lane % HEAD_SIZE) < HEAD_SIZE // 2
    width = x.shape[1]
    swapped = jnp.where(
        low, pltpu.roll(x, width - HEAD_SIZE // 2, 1), pltpu.roll(x, HEAD_SIZE // 2, 1)
    )
    return x * cosine + swapped * sine


def rotate_tables(positions):
    lane = jnp.arange(LANES, dtype=jnp.int32)
    frequency = 1.0 / rope_base ** (
        jnp.arange(0, HEAD_SIZE, 2, dtype=F32) / HEAD_SIZE
    )
    frequency = jnp.tile(frequency, LANES // (HEAD_SIZE // 2))
    angles = positions.astype(F32)[:, None] * frequency[None, :]
    sign = jnp.where((lane % HEAD_SIZE) < HEAD_SIZE // 2, -1.0, 1.0)
    return jnp.cos(angles), jnp.sin(angles) * sign[None, :]


def project_body(x_ref, w_ref, cos_ref, sin_ref, out_ref, *, query_width, rope_width):
    step = pl.program_id(0)
    width = w_ref.shape[1]
    tile = jnp.dot(x_ref[...], w_ref[...], preferred_element_type=F32)
    for i in range(width // LANES):
        part = tile[:, i * LANES : (i + 1) * LANES]
        column = step * width + i * LANES + lax.broadcasted_iota(jnp.int32, part.shape, 1)
        turned = rotate_tile(part, cos_ref[...], sin_ref[...])
        part = jnp.where(column < rope_width, turned, part)
        scale = jnp.where(column < query_width, HEAD_SIZE ** (-0.5), 1.0)
        out_ref[:, i * LANES : (i + 1) * LANES] = (part * scale).astype(BF16)


def project(x, w, cosine, sine, query_width, rope_width):
    rows, depth = x.shape
    width = w.shape[1] - query_width
    return pl.pallas_call(
        functools.partial(project_body, query_width=query_width, rope_width=rope_width),
        out_shape=jax.ShapeDtypeStruct((rows, w.shape[1]), BF16),
        grid=(w.shape[1] // width,),
        in_specs=[
            pl.BlockSpec((rows, depth), lambda i: (0, 0)),
            pl.BlockSpec((depth, width), lambda i: (0, i)),
            pl.BlockSpec((rows, LANES), lambda i: (0, 0)),
            pl.BlockSpec((rows, LANES), lambda i: (0, 0)),
        ],
        out_specs=pl.BlockSpec((rows, width), lambda i: (0, i)),
        name="project",
    )(x, w, cosine, sine)


def unrotate_body(x_ref, cos_ref, sin_ref, out_ref, *, rope_width):
    for i in range(x_ref.shape[1] // LANES):
        part = x_ref[:, i * LANES : (i + 1) * LANES].astype(F32)
        column = i * LANES + lax.broadcasted_iota(jnp.int32, part.shape, 1)
        turned = rotate_tile(part, cos_ref[...], -sin_ref[...])
        out_ref[:, i * LANES : (i + 1) * LANES] = jnp.where(
            column < rope_width, turned, part
        ).astype(BF16)


def unrotate(x, cosine, sine, rope_width):
    return pl.pallas_call(
        functools.partial(unrotate_body, rope_width=rope_width),
        out_shape=jax.ShapeDtypeStruct(x.shape, BF16),
        name="unrotate",
    )(x, cosine, sine)


def spread(tile_ref_value, entry):
    tile = tile_ref_value[:, (entry // 2) * LANES : (entry // 2 + 1) * LANES]
    lane = lax.broadcasted_iota(jnp.int32, tile.shape, 1)
    turned = pltpu.roll(tile.astype(F32), HEAD_SIZE, 1).astype(tile.dtype)
    zero = jnp.zeros_like(tile)
    first, second = (tile, turned) if entry % 2 == 0 else (turned, tile)
    return jnp.concatenate(
        [jnp.where(lane < HEAD_SIZE, first, zero), jnp.where(lane < HEAD_SIZE, zero, second)],
        axis=0,
    )


def lane_sums(e):
    total = e[:, :LANES]
    for i in range(1, e.shape[1] // LANES):
        total = total + e[:, i * LANES : (i + 1) * LANES]
    return total


def attend_body(
    meta, q_ref, kv_ref, row_ref, col_ref, o_ref, ob_ref, linv_ref, kk_ref, vv_ref, acc_ref, l_ref,
    *, heads, groups, span
):
    step = pl.program_id(0)
    key_block = meta[2 + step]
    per_group = heads // groups

    @pl.when(step == 0)
    def _():
        acc_ref[...] = jnp.zeros_like(acc_ref)
        l_ref[...] = jnp.zeros_like(l_ref)

    kv = kv_ref[...].reshape(span, 2 * groups * HEAD_SIZE)
    for g in range(groups):
        kk_ref[g] = spread(kv, g)
        vv_ref[g] = spread(kv, groups + g)

    def process(half, masked):
        if masked:
            mask = col_ref[0:1, :] <= row_ref[:, 0:1]
        for pair in range(heads // 2):
            g = 2 * pair // per_group
            q = q_ref[:, half, :, pair * LANES : (pair + 1) * LANES].reshape(span, LANES)
            scores = lax.dot_general(q, kk_ref[g], NT, preferred_element_type=F32)
            weights = []
            for i in range(2):
                e = jnp.exp(scores[:, i * span : (i + 1) * span])
                if masked:
                    e = jnp.where(mask, e, 0.0)
                l_ref[half, 2 * pair + i] += lane_sums(e)
                weights.append(e.astype(BF16))
            acc_ref[half, pair] += jnp.dot(
                jnp.concatenate(weights, axis=1), vv_ref[g], preferred_element_type=F32
            )

    for half in range(2):
        pl.when(key_block < meta[half])(functools.partial(process, half, False))
        pl.when(key_block == meta[half])(functools.partial(process, half, True))

    @pl.when(step == pl.num_programs(0) - 1)
    def _():
        n_slots, rows = q_ref.shape[0], q_ref.shape[2]
        for half in range(2):
            for pair in range(heads // 2):
                inverse = []
                for i in range(2):
                    sums = l_ref[half, 2 * pair + i]
                    inverse.append(1.0 / jnp.sum(sums, axis=1, keepdims=True))
                    across = jnp.sum(sums.T, axis=0, keepdims=True)
                    linv_ref[half, 2 * pair + i : 2 * pair + i + 1, :] = 1.0 / across
                acc = acc_ref[half, pair]
                lane = lax.broadcasted_iota(jnp.int32, acc.shape, 1)
                out = acc * jnp.where(lane < HEAD_SIZE, inverse[0], inverse[1])
                out = out.reshape(n_slots, rows, LANES)
                columns = slice(pair * LANES, (pair + 1) * LANES)
                o_ref[:, half, :, columns] = out
                ob_ref[:, half, :, columns] = out.astype(BF16)


def attend(meta, qkv, kv_all, row_pos, col_pos, heads, groups):
    n_slots, _, rows, _ = qkv.shape
    n_blocks = kv_all.shape[0] * 2
    span, width, kv_width = n_slots * rows, heads * HEAD_SIZE, 2 * groups * HEAD_SIZE
    whole = lambda j, m: (0, 0, 0, 0)
    flat = lambda j, m: (0, 0)
    shape = (n_slots, 2, rows, width)
    return pl.pallas_call(
        functools.partial(attend_body, heads=heads, groups=groups, span=span),
        out_shape=(
            jax.ShapeDtypeStruct(shape, F32),
            jax.ShapeDtypeStruct(shape, BF16),
            jax.ShapeDtypeStruct((2, heads, span), F32),
        ),
        grid_spec=pltpu.PrefetchScalarGridSpec(
            num_scalar_prefetch=1,
            grid=(n_blocks,),
            in_specs=[
                pl.BlockSpec(shape, whole),
                pl.BlockSpec((1, n_slots, 1, rows, kv_width), lambda j, m: (j // 2, 0, j % 2, 0, 0)),
                pl.BlockSpec(row_pos.shape, flat),
                pl.BlockSpec(col_pos.shape, flat),
            ],
            out_specs=[
                pl.BlockSpec(shape, whole),
                pl.BlockSpec(shape, whole),
                pl.BlockSpec((2, heads, span), lambda j, m: (0, 0, 0)),
            ],
            scratch_shapes=[
                pltpu.VMEM((groups, 2 * span, LANES), BF16),
                pltpu.VMEM((groups, 2 * span, LANES), BF16),
                pltpu.VMEM((2, heads // 2, span, LANES), F32),
                pltpu.VMEM((2, heads, span, LANES), F32),
            ],
        ),
        name="attend",
    )(meta, qkv, kv_all, row_pos, col_pos)


def attend_back_body(
    meta, q_ref, do_ref, kv_ref, linv_ref, delta_ref, row_ref, col_ref, cos_ref, sin_ref,
    dq_ref, dkv_ref, kk_ref, vv_ref, dq_acc, dkv_acc, *, heads, groups, span
):
    step = pl.program_id(0)
    key_block = meta[2 + step]
    per_group = heads // groups

    @pl.when(step == 0)
    def _():
        dq_acc[...] = jnp.zeros_like(dq_acc)

    kv = kv_ref[...].reshape(span, 2 * groups * HEAD_SIZE)
    for g in range(groups):
        kk_ref[g] = spread(kv, g)
        vv_ref[g] = spread(kv, groups + g)
    dkv_acc[...] = jnp.zeros_like(dkv_acc)

    def process(half, masked):
        if masked:
            mask = row_ref[:, 0:1] <= col_ref[0:1, :]
        lane = lax.broadcasted_iota(jnp.int32, (span, LANES), 1)
        for pair in range(heads // 2):
            g = 2 * pair // per_group
            columns = slice(pair * LANES, (pair + 1) * LANES)
            q = q_ref[:, half, :, columns].reshape(span, LANES)
            do = do_ref[:, half, :, columns].reshape(span, LANES)
            scores = lax.dot_general(kk_ref[g], q, NT, preferred_element_type=F32)
            d_probs = lax.dot_general(vv_ref[g], do, NT, preferred_element_type=F32)
            d_scores, d_keys, d_values = [], [], []
            for i in range(2):
                rows = slice(i * span, (i + 1) * span)
                head = slice(2 * pair + i, 2 * pair + i + 1)
                p = jnp.exp(scores[rows]) * linv_ref[half, head, :]
                if masked:
                    p = jnp.where(mask, p, 0.0)
                ds = (p * (d_probs[rows] - delta_ref[half, head, :])).astype(BF16)
                d_scores.append(ds)
                d_values.append(jnp.dot(p.astype(BF16), do, preferred_element_type=F32))
                d_keys.append(jnp.dot(ds, q, preferred_element_type=F32))
            dkv_acc[g] += jnp.where(lane < HEAD_SIZE, d_keys[0], d_keys[1])
            dkv_acc[groups + g] += jnp.where(lane < HEAD_SIZE, d_values[0], d_values[1])
            dq_acc[half, pair] += lax.dot_general(
                jnp.concatenate(d_scores, axis=0), kk_ref[g], TN, preferred_element_type=F32
            )

    for half in range(2):
        pl.when(key_block < meta[half])(functools.partial(process, half, False))
        pl.when(key_block == meta[half])(functools.partial(process, half, True))

    n_slots, rows = q_ref.shape[0], q_ref.shape[2]
    for t in range(groups):
        folds = []
        for i in (2 * t, 2 * t + 1):
            acc = dkv_acc[i]
            folds.append(acc + pltpu.roll(acc, HEAD_SIZE, 1))
        lane = lax.broadcasted_iota(jnp.int32, folds[0].shape, 1)
        out = jnp.where(lane < HEAD_SIZE, folds[0], folds[1]).astype(BF16)
        dkv_ref[0, :, 0, :, t * LANES : (t + 1) * LANES] = out.reshape(n_slots, rows, LANES)

    @pl.when(step == pl.num_programs(0) - 1)
    def _():
        for half in range(2):
            cosine = cos_ref[:, half].reshape(span, LANES)
            sine = sin_ref[:, half].reshape(span, LANES)
            for pair in range(heads // 2):
                dq = dq_acc[half, pair] * HEAD_SIZE ** (-0.5)
                out = rotate_tile(dq, cosine, -sine).astype(BF16)
                columns = slice(pair * LANES, (pair + 1) * LANES)
                dq_ref[:, half, :, columns] = out.reshape(n_slots, rows, LANES)


def attend_back(meta, qkv, do, kv_all, linv, delta, row_pos, col_pos, cosine, sine, heads, groups):
    n_slots, _, rows, _ = qkv.shape
    n_blocks = kv_all.shape[0] * 2
    span, width, kv_width = n_slots * rows, heads * HEAD_SIZE, 2 * groups * HEAD_SIZE
    whole = lambda j, m: (0, 0, 0, 0)
    flat = lambda j, m: (0, 0)
    cube = lambda j, m: (0, 0, 0)
    shape = (n_slots, 2, rows, width)
    block = pl.BlockSpec((1, n_slots, 1, rows, kv_width), lambda j, m: (j // 2, 0, j % 2, 0, 0))
    return pl.pallas_call(
        functools.partial(attend_back_body, heads=heads, groups=groups, span=span),
        out_shape=(
            jax.ShapeDtypeStruct(shape, BF16),
            jax.ShapeDtypeStruct(kv_all.shape, BF16),
        ),
        grid_spec=pltpu.PrefetchScalarGridSpec(
            num_scalar_prefetch=1,
            grid=(n_blocks,),
            in_specs=[
                pl.BlockSpec(shape, whole),
                pl.BlockSpec(shape, whole),
                block,
                pl.BlockSpec((2, heads, span), cube),
                pl.BlockSpec((2, heads, span), cube),
                pl.BlockSpec(row_pos.shape, flat),
                pl.BlockSpec(col_pos.shape, flat),
                pl.BlockSpec((n_slots, 2, rows, LANES), whole),
                pl.BlockSpec((n_slots, 2, rows, LANES), whole),
            ],
            out_specs=[pl.BlockSpec(shape, whole), block],
            scratch_shapes=[
                pltpu.VMEM((groups, 2 * span, LANES), BF16),
                pltpu.VMEM((groups, 2 * span, LANES), BF16),
                pltpu.VMEM((2, heads // 2, span, LANES), F32),
                pltpu.VMEM((2 * groups, span, LANES), F32),
            ],
        ),
        name="attend_back",
    )(meta, qkv, do, kv_all, linv, delta, row_pos, col_pos, cosine, sine)


def shards(
    hidden_in,
    pair_order,
    attn_gain,
    w_query,
    key_weight_matrix,
    value_weight_matrix,
    w_out,
    mlp_gain,
    w_gate,
    w_up,
    w_down,
    out_grad,
):
    n_ctx, n_fsdp = lax.axis_size("ctx"), lax.axis_size("fsdp")
    n_all = n_ctx * n_fsdp
    my_fsdp = lax.axis_index("fsdp")
    resident_rows, model_width = hidden_in.shape
    half_rows = resident_rows // 2
    span = half_rows * n_fsdp
    group_rows = resident_rows * n_fsdp
    heads, groups = QUERY_HEADS // n_fsdp, KEY_VALUE_HEADS // n_fsdp
    query_width, key_width = heads * HEAD_SIZE, groups * HEAD_SIZE
    kv_width = 2 * key_width
    hidden_units = w_gate.shape[1]
    unit_slice = hidden_units // n_fsdp
    weight_rows = w_gate.shape[0]

    labels = jnp.arange(n_ctx, dtype=jnp.int32)
    pair_block = jnp.sum(jnp.where(labels == lax.axis_index("ctx"), pair_order, 0))
    late_block = 2 * n_ctx - 1 - pair_block
    slot_owner = (my_fsdp - jnp.arange(n_fsdp, dtype=jnp.int32)) % n_fsdp
    block_pos = (
        slot_owner[:, None] * half_rows + jnp.arange(half_rows, dtype=jnp.int32)[None, :]
    )
    positions = jnp.stack(
        [pair_block * span + block_pos, late_block * span + block_pos], axis=1
    ).reshape(group_rows)
    cosine, sine = rotate_tables(positions)
    row_pos = jnp.broadcast_to(block_pos.reshape(span, 1), (span, LANES))
    col_pos = jnp.broadcast_to(block_pos.reshape(1, span), (8, span))
    key_blocks = jnp.stack([pair_order, 2 * n_ctx - 1 - pair_order], axis=1).reshape(2 * n_ctx)
    meta = jnp.concatenate([jnp.stack([pair_block, late_block]), key_blocks])

    both_gains = jnp.concatenate([attn_gain, mlp_gain]).reshape(1, 1, 2 * weight_rows)
    both_gains = lax.all_to_all(
        jnp.broadcast_to(both_gains, (n_all, 1, 2 * weight_rows)), BOTH, 0, 0, tiled=True
    )
    gain_one = both_gains[:, 0, :weight_rows].reshape(1, model_width).astype(F32)
    gain_two = both_gains[:, 0, weight_rows:].reshape(1, model_width).astype(F32)

    hidden_all = z_gather(hidden_in).astype(F32)

    def pick_attention(d):
        cut = lambda w, width: lax.dynamic_slice_in_dim(w, d * width, width, 1)
        return jnp.concatenate(
            [
                cut(w_query, query_width),
                cut(key_weight_matrix, key_width),
                cut(value_weight_matrix, key_width),
            ],
            axis=1,
        )

    w_qkv = ctx_gather(z_exchange(pick_attention).reshape(n_fsdp * weight_rows, -1))
    scale_all = lax.rsqrt(jnp.mean(hidden_all * hidden_all, axis=1, keepdims=True) + norm_eps)
    normed_one = (hidden_all * scale_all * gain_one).astype(BF16)
    qkv = project(normed_one, w_qkv, cosine, sine, query_width, query_width + key_width)
    kv_all = ctx_gather(qkv[:, query_width:]).reshape(n_ctx, n_fsdp, 2, half_rows, kv_width)
    q4 = qkv.reshape(n_fsdp, 2, half_rows, query_width + kv_width)[..., :query_width]

    to_slice = [(i, (i % n_ctx) * n_fsdp + i // n_ctx) for i in range(n_all)]
    from_slice = [(b, a) for a, b in to_slice]
    w_out_slice = ctx_gather(lax.ppermute(w_out, BOTH, to_slice))

    grad_all = z_gather(out_grad)

    def slice_of(w):
        pick = lambda d: lax.dynamic_slice_in_dim(w, d * unit_slice, unit_slice, 1)
        return ctx_gather(z_exchange(pick).reshape(n_fsdp * weight_rows, unit_slice))

    down_t = slice_of(w_down.T)
    gate_w = slice_of(w_gate)
    up_w = slice_of(w_up)

    o_full, o_b, linv = attend(meta, q4, kv_all, row_pos, col_pos, heads, groups)
    o_b2 = o_b.reshape(group_rows, query_width)
    residual = hidden_in.astype(F32)
    after_attn = residual + z_reduce(mm(o_b2, w_out_slice))
    scale_two = lax.rsqrt(jnp.mean(after_attn * after_attn, axis=1, keepdims=True) + norm_eps)
    unit_two = after_attn * scale_two
    normed_two = z_gather((unit_two * gain_two).astype(BF16))

    d_act = mm(grad_all, down_t)
    gate_proj = mm(normed_two, gate_w)
    up_proj = mm(normed_two, up_w)
    sigmoid_gate = jax.nn.sigmoid(gate_proj)
    activated = (gate_proj * sigmoid_gate * up_proj).astype(BF16)
    d_gate = (d_act * up_proj * sigmoid_gate * (1.0 + gate_proj * (1.0 - sigmoid_gate))).astype(
        BF16
    )
    d_up = (d_act * gate_proj * sigmoid_gate).astype(BF16)
    d_normed_two = z_reduce(mm(d_gate, gate_w, NT) + mm(d_up, up_w, NT))

    gain_two_grad = jnp.sum(d_normed_two * unit_two, axis=0)
    d_unit_two = d_normed_two * gain_two
    d_mixed = out_grad.astype(F32) + scale_two * (
        d_unit_two - unit_two * jnp.mean(d_unit_two * unit_two, axis=1, keepdims=True)
    )
    d_attn = z_gather(d_mixed.astype(BF16))

    ffn_grads = [
        ctx_reduce(mm(normed_two, d_gate, TN, BF16)),
        ctx_reduce(mm(normed_two, d_up, TN, BF16)),
        ctx_reduce(mm(grad_all, activated, TN, BF16)),
    ]
    result = after_attn + z_reduce(mm(activated, down_t, NT))

    d_o = mm(d_attn, w_out_slice, NT, BF16)
    grad_out_w = ctx_reduce(mm(o_b2, d_attn, TN, BF16))
    delta = jnp.sum(
        (d_o.astype(F32) * o_full.reshape(group_rows, query_width)).reshape(
            n_fsdp, 2, half_rows, heads, HEAD_SIZE
        ),
        axis=4,
    )
    delta = delta.transpose(1, 3, 0, 2).reshape(2, heads, span)
    dq, dkv_all = attend_back(
        meta,
        q4,
        d_o.reshape(n_fsdp, 2, half_rows, query_width),
        kv_all,
        linv,
        delta,
        row_pos,
        col_pos,
        cosine.reshape(n_fsdp, 2, half_rows, LANES),
        sine.reshape(n_fsdp, 2, half_rows, LANES),
        heads,
        groups,
    )
    dkv = ctx_reduce(dkv_all.reshape(n_ctx * group_rows, kv_width))
    dkv = unrotate(dkv, cosine, sine, key_width)
    d_qkv = jnp.concatenate([dq.reshape(group_rows, query_width), dkv], axis=1)
    d_normed_one = z_reduce(mm(d_qkv, w_qkv, NT))
    qkv_grads = ctx_reduce(mm(normed_one, d_qkv, TN, BF16))

    scale_one = lax.rsqrt(jnp.mean(residual * residual, axis=1, keepdims=True) + norm_eps)
    unit_one = residual * scale_one
    gain_one_grad = jnp.sum(d_normed_one * unit_one, axis=0)
    d_unit_one = d_normed_one * gain_one
    grad_in = d_mixed + scale_one * (
        d_unit_one - unit_one * jnp.mean(d_unit_one * unit_one, axis=1, keepdims=True)
    )

    def pieces_home(grads):
        rows_of = lambda d: lax.dynamic_slice_in_dim(grads, d * weight_rows, weight_rows, 0)
        return z_exchange(rows_of)

    def columns_home(grads):
        return pieces_home(grads).transpose(1, 0, 2).reshape(weight_rows, -1).astype(F32)

    gate_sum, up_sum, down_sum = [columns_home(g) for g in ffn_grads]
    out_sum = lax.ppermute(grad_out_w, BOTH, from_slice).astype(F32)
    qkv_home = pieces_home(qkv_grads).transpose(1, 0, 2).astype(F32)
    query_sum = qkv_home[:, :, :query_width].reshape(weight_rows, -1)
    key_sum = qkv_home[:, :, query_width : query_width + key_width].reshape(weight_rows, -1)
    value_sum = qkv_home[:, :, query_width + key_width :].reshape(weight_rows, -1)

    gain_grads = jnp.stack(
        [gain_one_grad.reshape(n_all, weight_rows), gain_two_grad.reshape(n_all, weight_rows)],
        axis=1,
    ).reshape(n_all, 1, 2 * weight_rows)
    gain_grads = jnp.sum(lax.all_to_all(gain_grads, BOTH, 0, 0, tiled=True), axis=0)
    return (
        result,
        grad_in,
        gain_grads[0, :weight_rows],
        query_sum,
        key_sum,
        value_sum,
        out_sum,
        gain_grads[0, weight_rows:],
        gate_sum,
        up_sum,
        down_sum.T,
    )


def solution(mesh):
    rows, columns, vector = P(BOTH, None), P(None, BOTH), P(BOTH)
    placed = (rows, P(), vector, rows, rows, rows, rows, vector, rows, rows, columns, rows)
    return jax.shard_map(
        shards,
        mesh=mesh,
        in_specs=placed,
        out_specs=(rows, rows, vector, rows, rows, rows, rows, vector, rows, rows, columns),
        check_vma=False,
    )
```

```python
import functools

import jax
import jax.numpy as jnp
from jax import lax
from jax.experimental import pallas as pl
from jax.experimental.pallas import tpu as pltpu
from jax.sharding import PartitionSpec as P

QUERY_HEADS = 32
KEY_VALUE_HEADS = 8
HEAD_SIZE = 64
LANES = 128

rope_base = 500000.0
norm_eps = 1e-05
BOTH = ("ctx", "fsdp")
BF16, F32 = jnp.bfloat16, jnp.float32


NT = (((1,), (1,)), ((), ()))
TN = (((0,), (0,)), ((), ()))
NN = (((1,), (0,)), ((), ()))


def mm(a, b, dims=NN, out=F32):
    return lax.dot_general(a, b, dims, preferred_element_type=F32).astype(out)


def shift_perm(n, s):
    return [(i, (i + s) % n) for i in range(n)]


def z_gather(x):
    n = lax.axis_size("fsdp")
    parts = [x] + [lax.ppermute(x, "fsdp", shift_perm(n, s)) for s in range(1, n)]
    return jnp.concatenate(parts, axis=0)


def z_reduce(partial):
    n = lax.axis_size("fsdp")
    rows = partial.shape[0] // n
    total = partial[:rows].astype(F32)
    for s in range(1, n):
        piece = partial[s * rows : (s + 1) * rows].astype(BF16)
        total = total + lax.ppermute(piece, "fsdp", shift_perm(n, -s)).astype(F32)
    return total


def z_exchange(pick):
    n, me = lax.axis_size("fsdp"), lax.axis_index("fsdp")
    own = pick(me)
    out = jnp.zeros((n,) + own.shape, own.dtype)
    out = lax.dynamic_update_index_in_dim(out, own, me, 0)
    for s in range(1, n):
        got = lax.ppermute(pick((me + s) % n), "fsdp", shift_perm(n, s))
        out = lax.dynamic_update_index_in_dim(out, got, (me - s) % n, 0)
    return out


def ctx_gather(x):
    return lax.all_gather(x, "ctx", axis=0, tiled=True)


def ctx_reduce(x):
    return lax.psum_scatter(x, "ctx", scatter_dimension=0, tiled=True)


def xor_slots(n):
    return list(range(0, n, 2)) + list(range(1, n, 2))


def xor_swap(x, bit):
    n = lax.axis_size("ctx")
    return lax.ppermute(x, "ctx", [(i, i ^ bit) for i in range(n)])


def bit_orders(n):
    bits = [1 << b for b in range(1, n.bit_length() - 1)]
    return bits, bits[::-1]


def xor_gather(x):
    n, rows = lax.axis_size("ctx"), x.shape[0] // 2
    halves = []
    for order, piece in zip(bit_orders(n), (x[:rows], x[rows:])):
        parts = {0: piece}
        for bit in order:
            parts.update({m ^ bit: xor_swap(part, bit) for m, part in list(parts.items())})
        halves.append(parts)
    mine = jnp.stack(
        [jnp.concatenate([half[m] for half in halves], axis=0) for m in xor_slots(n)[: n // 2]]
    )
    return jnp.concatenate([mine, xor_swap(mine, 1)], axis=0)


def xor_reduce(x):
    n, rows = lax.axis_size("ctx"), x.shape[1] // 2
    mine = (x[: n // 2].astype(F32) + xor_swap(x[n // 2 :], 1).astype(F32)).astype(BF16)
    done = []
    for order, cut in zip(bit_orders(n), (slice(None, rows), slice(rows, None))):
        parts = {m: mine[i, cut] for i, m in enumerate(xor_slots(n)[: n // 2])}
        for bit in order:
            away = sorted(m for m in parts if m & bit)
            got = xor_swap(jnp.stack([parts[m] for m in away]), bit)
            for i, m in enumerate(away):
                kept = parts[m ^ bit].astype(F32) + got[i].astype(F32)
                parts[m ^ bit] = kept.astype(BF16)
                del parts[m]
        done.append(parts[0])
    return jnp.concatenate(done, axis=0)


def after(x, *others):
    return lax.optimization_barrier((x,) + others)[0]


def rotate_tile(x, cosine, sine):
    lane = lax.broadcasted_iota(jnp.int32, x.shape, 1)
    low = (lane % HEAD_SIZE) < HEAD_SIZE // 2
    width = x.shape[1]
    swapped = jnp.where(
        low, pltpu.roll(x, width - HEAD_SIZE // 2, 1), pltpu.roll(x, HEAD_SIZE // 2, 1)
    )
    return x * cosine + swapped * sine


def rotate_tables(positions):
    lane = jnp.arange(LANES, dtype=jnp.int32)
    frequency = 1.0 / rope_base ** (
        jnp.arange(0, HEAD_SIZE, 2, dtype=F32) / HEAD_SIZE
    )
    frequency = jnp.tile(frequency, LANES // (HEAD_SIZE // 2))
    angles = positions.astype(F32)[:, None] * frequency[None, :]
    sign = jnp.where((lane % HEAD_SIZE) < HEAD_SIZE // 2, -1.0, 1.0)
    return jnp.cos(angles), jnp.sin(angles) * sign[None, :]


def project_body(x_ref, w_ref, cos_ref, sin_ref, out_ref, *, query_width, rope_width):
    step = pl.program_id(0)
    width = w_ref.shape[1]
    tile = jnp.dot(x_ref[...], w_ref[...], preferred_element_type=F32)
    for i in range(width // LANES):
        part = tile[:, i * LANES : (i + 1) * LANES]
        column = step * width + i * LANES + lax.broadcasted_iota(jnp.int32, part.shape, 1)
        turned = rotate_tile(part, cos_ref[...], sin_ref[...])
        part = jnp.where(column < rope_width, turned, part)
        scale = jnp.where(column < query_width, HEAD_SIZE ** (-0.5), 1.0)
        out_ref[:, i * LANES : (i + 1) * LANES] = (part * scale).astype(BF16)


def project(x, w, cosine, sine, query_width, rope_width):
    rows, depth = x.shape
    width = 2 * (rope_width - query_width)
    total = query_width + width
    return pl.pallas_call(
        functools.partial(project_body, query_width=query_width, rope_width=rope_width),
        out_shape=jax.ShapeDtypeStruct((rows, total), BF16),
        grid=(total // width,),
        in_specs=[
            pl.BlockSpec((rows, depth), lambda i: (0, 0)),
            pl.BlockSpec((depth, width), lambda i: (0, i)),
            pl.BlockSpec((rows, LANES), lambda i: (0, 0)),
            pl.BlockSpec((rows, LANES), lambda i: (0, 0)),
        ],
        out_specs=pl.BlockSpec((rows, width), lambda i: (0, i)),
        name="project",
    )(x, w, cosine, sine)


def unrotate_body(x_ref, cos_ref, sin_ref, out_ref, *, rope_width):
    for i in range(x_ref.shape[1] // LANES):
        part = x_ref[:, i * LANES : (i + 1) * LANES].astype(F32)
        column = i * LANES + lax.broadcasted_iota(jnp.int32, part.shape, 1)
        turned = rotate_tile(part, cos_ref[...], -sin_ref[...])
        out_ref[:, i * LANES : (i + 1) * LANES] = jnp.where(
            column < rope_width, turned, part
        ).astype(BF16)


def unrotate(x, cosine, sine, rope_width):
    return pl.pallas_call(
        functools.partial(unrotate_body, rope_width=rope_width),
        out_shape=jax.ShapeDtypeStruct(x.shape, BF16),
        name="unrotate",
    )(x, cosine, sine)


def spread(tile_ref_value, entry):
    tile = tile_ref_value[:, (entry // 2) * LANES : (entry // 2 + 1) * LANES]
    lane = lax.broadcasted_iota(jnp.int32, tile.shape, 1)
    turned = pltpu.roll(tile.astype(F32), HEAD_SIZE, 1).astype(tile.dtype)
    zero = jnp.zeros_like(tile)
    first, second = (tile, turned) if entry % 2 == 0 else (turned, tile)
    return jnp.concatenate(
        [jnp.where(lane < HEAD_SIZE, first, zero), jnp.where(lane < HEAD_SIZE, zero, second)],
        axis=0,
    )


def lane_sums(e):
    total = e[:, :LANES]
    for i in range(1, e.shape[1] // LANES):
        total = total + e[:, i * LANES : (i + 1) * LANES]
    return total


def attend_body(
    meta, q_ref, kv_ref, row_ref, col_ref, o_ref, ob_ref, linv_ref, kk_ref, vv_ref, acc_ref, l_ref,
    *, heads, groups, span
):
    step = pl.program_id(0)
    key_block = meta[2 + step]
    per_group = heads // groups

    @pl.when(step == 0)
    def _():
        acc_ref[...] = jnp.zeros_like(acc_ref)
        l_ref[...] = jnp.zeros_like(l_ref)

    kv = kv_ref[...].reshape(span, 2 * groups * HEAD_SIZE)
    for g in range(groups):
        kk_ref[g] = spread(kv, g)
        vv_ref[g] = spread(kv, groups + g)

    def process(half, masked):
        if masked:
            mask = col_ref[0:1, :] <= row_ref[:, 0:1]
        for pair in range(heads // 2):
            g = 2 * pair // per_group
            q = q_ref[:, half, :, pair * LANES : (pair + 1) * LANES].reshape(span, LANES)
            scores = lax.dot_general(q, kk_ref[g], NT, preferred_element_type=F32)
            weights = []
            for i in range(2):
                e = jnp.exp(scores[:, i * span : (i + 1) * span])
                if masked:
                    e = jnp.where(mask, e, 0.0)
                l_ref[half, 2 * pair + i] += lane_sums(e)
                weights.append(e.astype(BF16))
            acc_ref[half, pair] += jnp.dot(
                jnp.concatenate(weights, axis=1), vv_ref[g], preferred_element_type=F32
            )

    for half in range(2):
        pl.when(key_block < meta[half])(functools.partial(process, half, False))
        pl.when(key_block == meta[half])(functools.partial(process, half, True))

    @pl.when(step == pl.num_programs(0) - 1)
    def _():
        n_slots, rows = q_ref.shape[0], q_ref.shape[2]
        for half in range(2):
            for pair in range(heads // 2):
                inverse = []
                for i in range(2):
                    sums = l_ref[half, 2 * pair + i]
                    inverse.append(1.0 / jnp.sum(sums, axis=1, keepdims=True))
                    across = jnp.sum(sums.T, axis=0, keepdims=True)
                    linv_ref[half, 2 * pair + i : 2 * pair + i + 1, :] = 1.0 / across
                acc = acc_ref[half, pair]
                lane = lax.broadcasted_iota(jnp.int32, acc.shape, 1)
                out = acc * jnp.where(lane < HEAD_SIZE, inverse[0], inverse[1])
                out = out.reshape(n_slots, rows, LANES)
                columns = slice(pair * LANES, (pair + 1) * LANES)
                o_ref[:, half, :, columns] = out
                ob_ref[:, half, :, columns] = out.astype(BF16)


def attend(meta, qkv, kv_all, row_pos, col_pos, heads, groups):
    n_slots, _, rows, _ = qkv.shape
    n_blocks = kv_all.shape[0] * 2
    span, width, kv_width = n_slots * rows, heads * HEAD_SIZE, 2 * groups * HEAD_SIZE
    whole = lambda j, m: (0, 0, 0, 0)
    flat = lambda j, m: (0, 0)
    shape = (n_slots, 2, rows, width)
    return pl.pallas_call(
        functools.partial(attend_body, heads=heads, groups=groups, span=span),
        out_shape=(
            jax.ShapeDtypeStruct(shape, F32),
            jax.ShapeDtypeStruct(shape, BF16),
            jax.ShapeDtypeStruct((2, heads, span), F32),
        ),
        grid_spec=pltpu.PrefetchScalarGridSpec(
            num_scalar_prefetch=1,
            grid=(n_blocks,),
            in_specs=[
                pl.BlockSpec(shape, whole),
                pl.BlockSpec((1, n_slots, 1, rows, kv_width), lambda j, m: (j // 2, 0, j % 2, 0, 0)),
                pl.BlockSpec(row_pos.shape, flat),
                pl.BlockSpec(col_pos.shape, flat),
            ],
            out_specs=[
                pl.BlockSpec(shape, whole),
                pl.BlockSpec(shape, whole),
                pl.BlockSpec((2, heads, span), lambda j, m: (0, 0, 0)),
            ],
            scratch_shapes=[
                pltpu.VMEM((groups, 2 * span, LANES), BF16),
                pltpu.VMEM((groups, 2 * span, LANES), BF16),
                pltpu.VMEM((2, heads // 2, span, LANES), F32),
                pltpu.VMEM((2, heads, span, LANES), F32),
            ],
        ),
        name="attend",
    )(meta, qkv, kv_all, row_pos, col_pos)


def attend_back_body(
    meta, q_ref, do_ref, kv_ref, linv_ref, delta_ref, row_ref, col_ref, cos_ref, sin_ref,
    dq_ref, dkv_ref, kk_ref, vv_ref, dq_acc, dkv_acc, *, heads, groups, span
):
    step = pl.program_id(0)
    key_block = meta[2 + step]
    per_group = heads // groups

    @pl.when(step == 0)
    def _():
        dq_acc[...] = jnp.zeros_like(dq_acc)

    kv = kv_ref[...].reshape(span, 2 * groups * HEAD_SIZE)
    for g in range(groups):
        kk_ref[g] = spread(kv, g)
        vv_ref[g] = spread(kv, groups + g)
    dkv_acc[...] = jnp.zeros_like(dkv_acc)

    def process(half, masked):
        if masked:
            mask = row_ref[:, 0:1] <= col_ref[0:1, :]
        lane = lax.broadcasted_iota(jnp.int32, (span, LANES), 1)
        for pair in range(heads // 2):
            g = 2 * pair // per_group
            columns = slice(pair * LANES, (pair + 1) * LANES)
            q = q_ref[:, half, :, columns].reshape(span, LANES)
            do = do_ref[:, half, :, columns].reshape(span, LANES)
            scores = lax.dot_general(kk_ref[g], q, NT, preferred_element_type=F32)
            d_probs = lax.dot_general(vv_ref[g], do, NT, preferred_element_type=F32)
            d_scores, d_keys, d_values = [], [], []
            for i in range(2):
                rows = slice(i * span, (i + 1) * span)
                head = slice(2 * pair + i, 2 * pair + i + 1)
                p = jnp.exp(scores[rows]) * linv_ref[half, head, :]
                if masked:
                    p = jnp.where(mask, p, 0.0)
                ds = (p * (d_probs[rows] - delta_ref[half, head, :])).astype(BF16)
                d_scores.append(ds)
                d_values.append(jnp.dot(p.astype(BF16), do, preferred_element_type=F32))
                d_keys.append(jnp.dot(ds, q, preferred_element_type=F32))
            dkv_acc[g] += jnp.where(lane < HEAD_SIZE, d_keys[0], d_keys[1])
            dkv_acc[groups + g] += jnp.where(lane < HEAD_SIZE, d_values[0], d_values[1])
            dq_acc[half, pair] += lax.dot_general(
                jnp.concatenate(d_scores, axis=0), kk_ref[g], TN, preferred_element_type=F32
            )

    for half in range(2):
        pl.when(key_block < meta[half])(functools.partial(process, half, False))
        pl.when(key_block == meta[half])(functools.partial(process, half, True))

    n_slots, rows = q_ref.shape[0], q_ref.shape[2]
    for t in range(groups):
        folds = []
        for i in (2 * t, 2 * t + 1):
            acc = dkv_acc[i]
            folds.append(acc + pltpu.roll(acc, HEAD_SIZE, 1))
        lane = lax.broadcasted_iota(jnp.int32, folds[0].shape, 1)
        out = jnp.where(lane < HEAD_SIZE, folds[0], folds[1]).astype(BF16)
        dkv_ref[0, :, 0, :, t * LANES : (t + 1) * LANES] = out.reshape(n_slots, rows, LANES)

    @pl.when(step == pl.num_programs(0) - 1)
    def _():
        for half in range(2):
            cosine = cos_ref[:, half].reshape(span, LANES)
            sine = sin_ref[:, half].reshape(span, LANES)
            for pair in range(heads // 2):
                dq = dq_acc[half, pair] * HEAD_SIZE ** (-0.5)
                out = rotate_tile(dq, cosine, -sine).astype(BF16)
                columns = slice(pair * LANES, (pair + 1) * LANES)
                dq_ref[:, half, :, columns] = out.reshape(n_slots, rows, LANES)


def attend_back(meta, qkv, do, kv_all, linv, delta, row_pos, col_pos, cosine, sine, heads, groups):
    n_slots, _, rows, _ = qkv.shape
    n_blocks = kv_all.shape[0] * 2
    span, width, kv_width = n_slots * rows, heads * HEAD_SIZE, 2 * groups * HEAD_SIZE
    whole = lambda j, m: (0, 0, 0, 0)
    flat = lambda j, m: (0, 0)
    cube = lambda j, m: (0, 0, 0)
    shape = (n_slots, 2, rows, width)
    block = pl.BlockSpec((1, n_slots, 1, rows, kv_width), lambda j, m: (j // 2, 0, j % 2, 0, 0))
    return pl.pallas_call(
        functools.partial(attend_back_body, heads=heads, groups=groups, span=span),
        out_shape=(
            jax.ShapeDtypeStruct(shape, BF16),
            jax.ShapeDtypeStruct(kv_all.shape, BF16),
        ),
        grid_spec=pltpu.PrefetchScalarGridSpec(
            num_scalar_prefetch=1,
            grid=(n_blocks,),
            in_specs=[
                pl.BlockSpec(shape, whole),
                pl.BlockSpec(shape, whole),
                block,
                pl.BlockSpec((2, heads, span), cube),
                pl.BlockSpec((2, heads, span), cube),
                pl.BlockSpec(row_pos.shape, flat),
                pl.BlockSpec(col_pos.shape, flat),
                pl.BlockSpec((n_slots, 2, rows, LANES), whole),
                pl.BlockSpec((n_slots, 2, rows, LANES), whole),
            ],
            out_specs=[pl.BlockSpec(shape, whole), block],
            scratch_shapes=[
                pltpu.VMEM((groups, 2 * span, LANES), BF16),
                pltpu.VMEM((groups, 2 * span, LANES), BF16),
                pltpu.VMEM((2, heads // 2, span, LANES), F32),
                pltpu.VMEM((2 * groups, span, LANES), F32),
            ],
        ),
        name="attend_back",
    )(meta, qkv, do, kv_all, linv, delta, row_pos, col_pos, cosine, sine)


def shards(
    hidden_in,
    pair_order,
    attn_gain,
    w_query,
    key_weight_matrix,
    value_weight_matrix,
    w_out,
    mlp_gain,
    w_gate,
    w_up,
    w_down,
    out_grad,
):
    n_ctx, n_fsdp = lax.axis_size("ctx"), lax.axis_size("fsdp")
    n_all = n_ctx * n_fsdp
    my_fsdp = lax.axis_index("fsdp")
    resident_rows, model_width = hidden_in.shape
    half_rows = resident_rows // 2
    span = half_rows * n_fsdp
    group_rows = resident_rows * n_fsdp
    heads, groups = QUERY_HEADS // n_fsdp, KEY_VALUE_HEADS // n_fsdp
    query_width, key_width = heads * HEAD_SIZE, groups * HEAD_SIZE
    kv_width = 2 * key_width
    hidden_units = w_gate.shape[1]
    unit_slice = hidden_units // n_fsdp
    weight_rows = w_gate.shape[0]

    labels = jnp.arange(n_ctx, dtype=jnp.int32)
    pair_block = jnp.sum(jnp.where(labels == lax.axis_index("ctx"), pair_order, 0))
    late_block = 2 * n_ctx - 1 - pair_block
    slot_owner = (my_fsdp - jnp.arange(n_fsdp, dtype=jnp.int32)) % n_fsdp
    block_pos = (
        slot_owner[:, None] * half_rows + jnp.arange(half_rows, dtype=jnp.int32)[None, :]
    )
    positions = jnp.stack(
        [pair_block * span + block_pos, late_block * span + block_pos], axis=1
    ).reshape(group_rows)
    cosine, sine = rotate_tables(positions)
    row_pos = jnp.broadcast_to(block_pos.reshape(span, 1), (span, LANES))
    col_pos = jnp.broadcast_to(block_pos.reshape(1, span), (8, span))
    slot_device = lax.axis_index("ctx") ^ jnp.array(xor_slots(n_ctx), jnp.int32)
    slot_block = jnp.sum(
        jnp.where(slot_device[:, None] == labels[None, :], pair_order[None, :], 0), axis=1
    )
    key_blocks = jnp.stack([slot_block, 2 * n_ctx - 1 - slot_block], axis=1).reshape(2 * n_ctx)
    meta = jnp.concatenate([jnp.stack([pair_block, late_block]), key_blocks])

    hidden_all = z_gather(hidden_in).astype(F32)

    gain_columns = jnp.pad(jnp.stack([attn_gain, mlp_gain], axis=1), ((0, 0), (0, LANES - 2)))

    def pick_attention(d):
        cut = lambda w, width: lax.dynamic_slice_in_dim(w, d * width, width, 1)
        return jnp.concatenate(
            [
                cut(w_query, query_width),
                cut(key_weight_matrix, key_width),
                cut(value_weight_matrix, key_width),
                gain_columns,
            ],
            axis=1,
        )

    w_first = ctx_gather(z_exchange(pick_attention).reshape(n_fsdp * weight_rows, -1))
    w_qkv = w_first[:, : query_width + kv_width]
    gain_rows = w_first[:, query_width + kv_width :].astype(F32).T[:2]
    gain_one, gain_two = gain_rows[0:1], gain_rows[1:2]
    scale_all = lax.rsqrt(jnp.mean(hidden_all * hidden_all, axis=1, keepdims=True) + norm_eps)
    unit_one_all = hidden_all * scale_all
    normed_one = (unit_one_all * gain_one).astype(BF16)
    qkv = project(normed_one, w_first, cosine, sine, query_width, query_width + key_width)
    kv_all = xor_gather(qkv[:, query_width:]).reshape(n_ctx, n_fsdp, 2, half_rows, kv_width)
    q4 = qkv.reshape(n_fsdp, 2, half_rows, query_width + kv_width)[..., :query_width]

    to_slice = [(i, (i % n_ctx) * n_fsdp + i // n_ctx) for i in range(n_all)]
    from_slice = [(b, a) for a, b in to_slice]
    w_out_slice = ctx_gather(lax.ppermute(w_out, BOTH, to_slice))

    grad_all = z_gather(out_grad)

    def slice_of(w):
        pick = lambda d: lax.dynamic_slice_in_dim(w, d * unit_slice, unit_slice, 1)
        return ctx_gather(z_exchange(pick).reshape(n_fsdp * weight_rows, unit_slice))

    down_t = slice_of(w_down.T)
    gate_w = slice_of(w_gate)
    up_w = slice_of(w_up)

    o_full, o_b, linv = attend(meta, q4, kv_all, row_pos, col_pos, heads, groups)
    o_b2 = o_b.reshape(group_rows, query_width)
    residual = hidden_in.astype(F32)
    after_attn = residual + z_reduce(mm(o_b2, w_out_slice))
    scale_two = lax.rsqrt(jnp.mean(after_attn * after_attn, axis=1, keepdims=True) + norm_eps)
    unit_two = after_attn * scale_two
    normed_two = z_gather((unit_two * gain_two).astype(BF16))

    d_act = mm(grad_all, down_t)
    gate_proj = mm(normed_two, gate_w)
    up_proj = mm(normed_two, up_w)
    sigmoid_gate = jax.nn.sigmoid(gate_proj)
    activated = (gate_proj * sigmoid_gate * up_proj).astype(BF16)
    d_gate = (d_act * up_proj * sigmoid_gate * (1.0 + gate_proj * (1.0 - sigmoid_gate))).astype(
        BF16
    )
    d_up = (d_act * gate_proj * sigmoid_gate).astype(BF16)
    d_normed_two = z_reduce(mm(d_gate, gate_w, NT) + mm(d_up, up_w, NT))

    gain_two_grad = jnp.sum(d_normed_two * unit_two, axis=0)
    d_unit_two = d_normed_two * gain_two
    d_mixed = out_grad.astype(F32) + scale_two * (
        d_unit_two - unit_two * jnp.mean(d_unit_two * unit_two, axis=1, keepdims=True)
    )
    d_attn = z_gather(d_mixed.astype(BF16))

    ffn_partials = [
        mm(normed_two, d_gate, TN, BF16),
        mm(normed_two, d_up, TN, BF16),
        mm(grad_all, activated, TN, BF16),
    ]
    ffn_grads = [ctx_reduce(g) for g in ffn_partials]
    d_attn = after(d_attn, *ffn_partials)
    result = after_attn + z_reduce(mm(after(activated, d_attn), down_t, NT))

    d_o = mm(d_attn, w_out_slice, NT, BF16)
    me_ctx = lax.axis_index("ctx")
    out_partial = mm(o_b2, d_attn, TN, BF16).reshape(n_ctx, weight_rows, model_width)
    grad_out_w = xor_reduce(
        jnp.stack(
            [lax.dynamic_index_in_dim(out_partial, me_ctx ^ m, 0, False) for m in xor_slots(n_ctx)]
        )
    )
    delta = jnp.sum(
        (d_o.astype(F32) * o_full.reshape(group_rows, query_width)).reshape(
            n_fsdp, 2, half_rows, heads, HEAD_SIZE
        ),
        axis=4,
    )
    delta = delta.transpose(1, 3, 0, 2).reshape(2, heads, span)
    dq, dkv_all = attend_back(
        meta,
        q4,
        d_o.reshape(n_fsdp, 2, half_rows, query_width),
        kv_all,
        linv,
        delta,
        row_pos,
        col_pos,
        cosine.reshape(n_fsdp, 2, half_rows, LANES),
        sine.reshape(n_fsdp, 2, half_rows, LANES),
        heads,
        groups,
    )
    dkv = xor_reduce(dkv_all.reshape(n_ctx, group_rows, kv_width))
    dkv = unrotate(dkv, cosine, sine, key_width)
    d_qkv = jnp.concatenate([dq.reshape(group_rows, query_width), dkv], axis=1)
    d_normed_partial = mm(d_qkv, w_qkv, NT)
    d_normed_one = z_reduce(d_normed_partial)
    gain_one_grad = jnp.sum(d_normed_partial * unit_one_all, axis=0)
    gain_grads = jnp.pad(
        jnp.stack([gain_one_grad, gain_two_grad], axis=1), ((0, 0), (0, LANES - 2))
    ).astype(BF16)
    block = n_fsdp * weight_rows
    normed_xor = jnp.concatenate(
        [
            lax.dynamic_slice_in_dim(normed_one, (me_ctx ^ m) * block, block, 1)
            for m in xor_slots(n_ctx)
        ],
        axis=1,
    )
    qkv_partial = mm(normed_xor, d_qkv, TN, BF16).reshape(n_ctx, block, -1)
    gain_slots = jnp.stack(
        [
            lax.dynamic_slice_in_dim(gain_grads, (me_ctx ^ m) * block, block, 0)
            for m in xor_slots(n_ctx)
        ]
    )
    qkv_grads = xor_reduce(jnp.concatenate([qkv_partial, gain_slots], axis=2))

    scale_one = lax.rsqrt(jnp.mean(residual * residual, axis=1, keepdims=True) + norm_eps)
    unit_one = residual * scale_one
    d_unit_one = d_normed_one * gain_one
    grad_in = d_mixed + scale_one * (
        d_unit_one - unit_one * jnp.mean(d_unit_one * unit_one, axis=1, keepdims=True)
    )

    def pieces_home(grads):
        rows_of = lambda d: lax.dynamic_slice_in_dim(grads, d * weight_rows, weight_rows, 0)
        yield my_fsdp, rows_of(my_fsdp)
        for s in range(1, n_fsdp):
            piece = rows_of((my_fsdp + s) % n_fsdp)
            yield (my_fsdp - s) % n_fsdp, lax.ppermute(piece, "fsdp", shift_perm(n_fsdp, s))

    def columns_home(pieces, width):
        out = jnp.zeros((weight_rows, width * n_fsdp), F32)
        for owner, piece in pieces:
            out = lax.dynamic_update_slice_in_dim(out, piece.astype(F32), owner * width, 1)
        return out

    gate_sum, up_sum, down_sum = [columns_home(pieces_home(g), unit_slice) for g in ffn_grads]
    out_sum = lax.ppermute(grad_out_w, BOTH, from_slice).astype(F32)
    qkv_home = list(pieces_home(qkv_grads))

    def part_home(start, width):
        return columns_home([(o, p[:, start : start + width]) for o, p in qkv_home], width)

    query_sum = part_home(0, query_width)
    key_sum = part_home(query_width, key_width)
    value_sum = part_home(query_width + key_width, key_width)
    gain_sums = sum(p[:, query_width + kv_width :].astype(F32) for _, p in qkv_home)
    return (
        result,
        grad_in,
        gain_sums[:, 0],
        query_sum,
        key_sum,
        value_sum,
        out_sum,
        gain_sums[:, 1],
        gate_sum,
        up_sum,
        down_sum.T,
    )


def solution(mesh):
    rows, columns, vector = P(BOTH, None), P(None, BOTH), P(BOTH)
    placed = (rows, P(), vector, rows, rows, rows, rows, vector, rows, rows, columns, rows)
    return jax.shard_map(
        shards,
        mesh=mesh,
        in_specs=placed,
        out_specs=(rows, rows, vector, rows, rows, rows, rows, vector, rows, rows, columns),
        check_vma=False,
    )
```

```python
import functools

import jax
import jax.numpy as jnp
from jax import lax
from jax.experimental import pallas as pl
from jax.experimental.pallas import tpu as pltpu
from jax.sharding import PartitionSpec as P


QUERY_HEADS = 32
KEY_VALUE_HEADS = 8
HEAD_SIZE = 64
LANES = 128

rope_base = 500000.0
norm_eps = 1e-05
CTX, FSDP = BOTH = ("ctx", "fsdp")
BF16, F32 = jnp.bfloat16, jnp.float32


NT = (((1,), (1,)), ((), ()))
TN = (((0,), (0,)), ((), ()))
NN = (((1,), (0,)), ((), ()))


def mm(a, b, dims=NN, out=F32):
    return lax.dot_general(a, b, dims, preferred_element_type=F32).astype(out)


def shift_perm(n, s):
    return [(i, (i + s) % n) for i in range(n)]


def z_gather(x):
    n = lax.axis_size(FSDP)
    parts = [x] + [lax.ppermute(x, FSDP, shift_perm(n, s)) for s in range(1, n)]
    return jnp.concatenate(parts, axis=0)


def z_reduce(partial):
    n = lax.axis_size(FSDP)
    rows = partial.shape[0] // n
    total = partial[:rows].astype(F32)
    for s in range(1, n):
        piece = partial[s * rows : (s + 1) * rows].astype(BF16)
        total = total + lax.ppermute(piece, FSDP, shift_perm(n, -s)).astype(F32)
    return total


def z_exchange(x):
    return lax.all_to_all(x, FSDP, 0, 0, tiled=True)


def z_sum(pick):
    n, me = lax.axis_size(FSDP), lax.axis_index(FSDP)
    total = pick(me).astype(F32)
    for s in range(1, n):
        got = lax.ppermute(pick((me + s) % n), FSDP, shift_perm(n, s))
        total = total + got.astype(F32)
    return total


def z_spread(pick):
    n, me = lax.axis_size(FSDP), lax.axis_index(FSDP)
    own = pick(me)
    out = jnp.zeros((n,) + own.shape, own.dtype)
    out = lax.dynamic_update_index_in_dim(out, own, me, 0)
    for s in range(1, n):
        got = lax.ppermute(pick((me + s) % n), FSDP, shift_perm(n, s))
        out = lax.dynamic_update_index_in_dim(out, got, (me - s) % n, 0)
    return out


def ctx_gather(x):
    return lax.all_gather(x, CTX, axis=0, tiled=True)


def ctx_reduce(x):
    return lax.psum_scatter(x, CTX, scatter_dimension=0, tiled=True)


def xor_slots(n):
    return list(range(0, n, 2)) + list(range(1, n, 2))


def xor_swap(x, bit):
    n = lax.axis_size(CTX)
    return lax.ppermute(x, CTX, [(i, i ^ bit) for i in range(n)])


def bit_orders(n):
    bits = [1 << b for b in range(1, n.bit_length() - 1)]
    return bits, bits[::-1]


def xor_gather(x):
    n, rows = lax.axis_size(CTX), x.shape[0] // 2
    halves = []
    for order, piece in zip(bit_orders(n), (x[:rows], x[rows:])):
        parts = {0: piece}
        for bit in order:
            parts.update({m ^ bit: xor_swap(part, bit) for m, part in list(parts.items())})
        halves.append(parts)
    mine = jnp.stack(
        [jnp.concatenate([half[m] for half in halves], axis=0) for m in xor_slots(n)[: n // 2]]
    )
    return jnp.concatenate([mine, xor_swap(mine, 1)], axis=0)


def xor_reduce(x):
    n, rows = lax.axis_size(CTX), x.shape[1] // 2
    got = xor_swap(x[n // 2 :], 1)
    mine = (x[: n // 2].astype(F32) + got.astype(F32)).astype(BF16)
    done = []
    for order, cut in zip(bit_orders(n), (slice(None, rows), slice(rows, None))):
        parts = {m: mine[i, cut] for i, m in enumerate(xor_slots(n)[: n // 2])}
        for bit in order:
            away = sorted(m for m in parts if m & bit)
            got = xor_swap(jnp.stack([parts[m] for m in away]), bit)
            for i, m in enumerate(away):
                kept = parts[m ^ bit].astype(F32) + got[i].astype(F32)
                parts[m ^ bit] = kept if len(away) == 1 else kept.astype(BF16)
                del parts[m]
        done.append(parts[0])
    return jnp.concatenate(done, axis=0)


def after(x, *others):
    return lax.optimization_barrier((x,) + others)[0]


def rotate_tile(x, cosine, sine):
    lane = lax.broadcasted_iota(jnp.int32, x.shape, 1)
    low = (lane % HEAD_SIZE) < HEAD_SIZE // 2
    width = x.shape[1]
    swapped = jnp.where(
        low, pltpu.roll(x, width - HEAD_SIZE // 2, 1), pltpu.roll(x, HEAD_SIZE // 2, 1)
    )
    return x * cosine + swapped * sine


def rotate_tables(positions):
    lane = jnp.arange(LANES, dtype=jnp.int32)
    frequency = 1.0 / rope_base ** (
        jnp.arange(0, HEAD_SIZE, 2, dtype=F32) / HEAD_SIZE
    )
    frequency = jnp.tile(frequency, LANES // (HEAD_SIZE // 2))
    angles = positions.astype(F32)[:, None] * frequency[None, :]
    sign = jnp.where((lane % HEAD_SIZE) < HEAD_SIZE // 2, -1.0, 1.0)
    return jnp.cos(angles), jnp.sin(angles) * sign[None, :]


def project_body(
    x_ref, gain_ref, w_ref, cos_ref, sin_ref, normed_ref, out_ref, flat_ref, *, query_width, rows
):
    @pl.when(pl.program_id(0) == 0)
    def _():
        flat_ref[...] = w_ref[:, :, :rows, :].reshape(flat_ref.shape)

    x = x_ref[...].astype(F32)
    scale = lax.rsqrt(jnp.mean(x * x, axis=1, keepdims=True) + norm_eps)
    normed = (x * scale * gain_ref[...]).astype(BF16)
    normed_ref[...] = normed
    tile = jnp.dot(normed, flat_ref[...], preferred_element_type=F32)
    for i in range(out_ref.shape[1] // LANES):
        part = tile[:, i * LANES : (i + 1) * LANES]
        column = i * LANES + lax.broadcasted_iota(jnp.int32, part.shape, 1)
        turned = rotate_tile(part, cos_ref[...], sin_ref[...])
        part = jnp.where(column < query_width + HEAD_SIZE, turned, part)
        scale = jnp.where(column < query_width, HEAD_SIZE ** (-0.5), 1.0)
        out_ref[:, i * LANES : (i + 1) * LANES] = (part * scale).astype(BF16)


def project(x, gain, w, cosine, sine, query_width, w_rows):
    rows, depth = x.shape
    width = w.shape[3]
    tile = min(rows, 256)
    return pl.pallas_call(
        functools.partial(project_body, query_width=query_width, rows=w_rows),
        out_shape=(
            jax.ShapeDtypeStruct((rows, depth), BF16),
            jax.ShapeDtypeStruct((rows, width), BF16),
            jax.ShapeDtypeStruct((depth, width), BF16),
        ),
        grid=(rows // tile,),
        in_specs=[
            pl.BlockSpec((tile, depth), lambda i: (i, 0)),
            pl.BlockSpec((1, depth), lambda i: (0, 0)),
            pl.BlockSpec(w.shape, lambda i: (0, 0, 0, 0)),
            pl.BlockSpec((tile, LANES), lambda i: (i, 0)),
            pl.BlockSpec((tile, LANES), lambda i: (i, 0)),
        ],
        out_specs=[
            pl.BlockSpec((tile, depth), lambda i: (i, 0)),
            pl.BlockSpec((tile, width), lambda i: (i, 0)),
            pl.BlockSpec((depth, width), lambda i: (0, 0)),
        ],
        name="project",
    )(x, gain, w, cosine, sine)


def unrotate_body(x_ref, cos_ref, sin_ref, out_ref):
    part = x_ref[...]
    lane = lax.broadcasted_iota(jnp.int32, part.shape, 1)
    turned = rotate_tile(part, cos_ref[...], -sin_ref[...])
    out_ref[...] = jnp.where(lane < HEAD_SIZE, turned, part).astype(BF16)


def unrotate(x, cosine, sine):
    return pl.pallas_call(
        unrotate_body, out_shape=jax.ShapeDtypeStruct(x.shape, BF16), name="unrotate"
    )(x, cosine, sine)


def stack_heads(x, heads, high):
    out = []
    for h in range(heads):
        tile = x[:, (h // 2) * LANES : (h // 2 + 1) * LANES].astype(F32)
        if (h % 2 == 1) != high:
            tile = pltpu.roll(tile, HEAD_SIZE, 1)
        lane = lax.broadcasted_iota(jnp.int32, tile.shape, 1)
        out.append(jnp.where((lane >= HEAD_SIZE) == high, tile, 0.0))
    return jnp.concatenate(out, axis=0)


def join_heads(stacked, heads, high):
    rows = stacked.shape[0] // heads
    for pair in range(heads // 2):
        even = stacked[2 * pair * rows : (2 * pair + 1) * rows]
        odd = stacked[(2 * pair + 1) * rows : (2 * pair + 2) * rows]
        if high:
            even = pltpu.roll(even, HEAD_SIZE, 1)
        else:
            odd = pltpu.roll(odd, HEAD_SIZE, 1)
        lane = lax.broadcasted_iota(jnp.int32, even.shape, 1)
        yield slice(pair * LANES, (pair + 1) * LANES), jnp.where(lane < HEAD_SIZE, even, odd)


def lane_sums(e):
    total = e[:, :LANES]
    for i in range(1, e.shape[1] // LANES):
        total = total + e[:, i * LANES : (i + 1) * LANES]
    return total


def across(x):
    return jnp.sum(x.T, axis=0, keepdims=True)


def items(meta, step, n_blocks):
    early = meta[step]
    place = lambda block: meta[n_blocks // 2 + block]
    for half in range(2):
        yield half, place(early if half == 0 else n_blocks - 1 - early), True
    for t in range(n_blocks - 1):
        late = t >= early
        yield late.astype(jnp.int32), place(jnp.where(late, t - early, t)), False


def attend_body(
    meta, q_ref, kv_ref, row_ref, col_ref, o_ref, ob_ref, linv_ref, qs_ref, acc_ref, l_ref, *, heads
):
    step = pl.program_id(0)
    n_slots, n_pairs, _, rows, _ = kv_ref.shape
    for half in range(2):
        qs_ref[half] = stack_heads(q_ref[0, half], heads, False).astype(BF16)
    acc_ref[...] = jnp.zeros_like(acc_ref)
    l_ref[...] = jnp.zeros_like(l_ref)
    for half, place, diagonal in items(meta, step, 2 * n_pairs):
        kv = kv_ref[:, place // 2, place % 2].reshape(n_slots * rows, LANES)
        e = jnp.exp(lax.dot_general(qs_ref[half], kv, NT, preferred_element_type=F32))
        if diagonal:
            e = jnp.where(col_ref[0:1, :] <= row_ref[:, 0:1], e, 0.0)
        l_ref[half] += lane_sums(e)
        acc_ref[half] += jnp.dot(e.astype(BF16), kv, preferred_element_type=F32)
    for half in range(2):
        sums = l_ref[half]
        linv_ref[0, half : half + 1, :] = 1.0 / across(sums)
        out = acc_ref[half] * (1.0 / jnp.sum(sums, axis=1, keepdims=True))
        for columns, tile in join_heads(out, heads, True):
            o_ref[0, half, :, columns] = tile
            ob_ref[0, half, :, columns] = tile.astype(BF16)


def attend_back_body(
    meta, q_ref, do_ref, o_ref, kv_ref, linv_ref, row_ref, col_ref, cos_ref, sin_ref,
    dq_ref, dkv_ref, qd_ref, delta_ref, dq_acc, dkv_acc, *, heads
):
    step = pl.program_id(0)
    n_slots, n_pairs, _, rows, _ = kv_ref.shape
    span, tall = n_slots * rows, heads * rows

    @pl.when(step == 0)
    def _():
        dkv_acc[...] = jnp.zeros_like(dkv_acc)

    dq_acc[...] = jnp.zeros_like(dq_acc)
    for half in range(2):
        qd_ref[half, :tall] = stack_heads(q_ref[0, half], heads, False).astype(BF16)
        do = stack_heads(do_ref[0, half], heads, True)
        qd_ref[half, tall:] = do.astype(BF16)
        delta_ref[half] = across(do * stack_heads(o_ref[0, half], heads, True))
    for half, place, diagonal in items(meta, step, 2 * n_pairs):
        kv = kv_ref[:, place // 2, place % 2].reshape(span, LANES)
        e = jnp.exp(lax.dot_general(kv, qd_ref[half, :tall], NT, preferred_element_type=F32))
        p = e * linv_ref[0, pl.ds(half, 1), :]
        if diagonal:
            p = jnp.where(row_ref[:, 0:1] <= col_ref[0:1, :], p, 0.0)
        dp = lax.dot_general(kv, qd_ref[half, tall:], NT, preferred_element_type=F32)
        ds = (p * (dp - delta_ref[half])).astype(BF16)
        dkv_acc[place] += jnp.dot(
            jnp.concatenate([ds, p.astype(BF16)], axis=1), qd_ref[half], preferred_element_type=F32
        )
        dq_acc[half] += lax.dot_general(ds, kv, TN, preferred_element_type=F32)
    for half in range(2):
        for columns, tile in join_heads(dq_acc[half] * HEAD_SIZE ** (-0.5), heads, False):
            turned = rotate_tile(tile, cos_ref[0, half], -sin_ref[0, half])
            dq_ref[0, half, :, columns] = turned.astype(BF16)

    @pl.when(step == pl.num_programs(0) - 1)
    def _():
        for place in range(2 * n_pairs):
            dkv_ref[:, place // 2, place % 2] = (
                dkv_acc[place].astype(BF16).reshape(n_slots, rows, LANES)
            )


def attention_specs(kv_all):
    _, _, _, rows, _ = kv_all.shape
    pair = lambda w: pl.BlockSpec((1, 2, rows, w), lambda j, m: (j, 0, 0, 0))
    held = lambda x: pl.BlockSpec(x.shape, lambda j, m: (0,) * len(x.shape))
    return pair, held


def attend(meta, qkv, kv_all, row_pos, col_pos, heads):
    _, n_pairs, _, rows, _ = kv_all.shape
    width = heads * HEAD_SIZE
    pair, held = attention_specs(kv_all)
    across_spec = pl.BlockSpec((1, 2, heads * rows), lambda j, m: (j, 0, 0))
    return pl.pallas_call(
        functools.partial(attend_body, heads=heads),
        out_shape=(
            jax.ShapeDtypeStruct((n_pairs, 2, rows, width), F32),
            jax.ShapeDtypeStruct((n_pairs, 2, rows, width), BF16),
            jax.ShapeDtypeStruct((n_pairs, 2, heads * rows), F32),
        ),
        grid_spec=pltpu.PrefetchScalarGridSpec(
            num_scalar_prefetch=1,
            grid=(n_pairs,),
            in_specs=[pair(width), held(kv_all), held(row_pos), held(col_pos)],
            out_specs=[pair(width), pair(width), across_spec],
            scratch_shapes=[
                pltpu.VMEM((2, heads * rows, LANES), BF16),
                pltpu.VMEM((2, heads * rows, LANES), F32),
                pltpu.VMEM((2, heads * rows, LANES), F32),
            ],
        ),
        name="attend",
    )(meta, qkv, kv_all, row_pos, col_pos)


def attend_back(meta, qkv, do, o, kv_all, linv, row_pos, col_pos, cosine, sine, heads):
    n_slots, n_pairs, _, rows, _ = kv_all.shape
    width, tall = heads * HEAD_SIZE, heads * rows
    pair, held = attention_specs(kv_all)
    across_spec = pl.BlockSpec((1, 2, tall), lambda j, m: (j, 0, 0))
    return pl.pallas_call(
        functools.partial(attend_back_body, heads=heads),
        out_shape=(
            jax.ShapeDtypeStruct((n_pairs, 2, rows, width), BF16),
            jax.ShapeDtypeStruct(kv_all.shape, BF16),
        ),
        grid_spec=pltpu.PrefetchScalarGridSpec(
            num_scalar_prefetch=1,
            grid=(n_pairs,),
            in_specs=[
                pair(width), pair(width), pair(width), held(kv_all), across_spec,
                held(row_pos), held(col_pos), pair(LANES), pair(LANES),
            ],
            out_specs=[pair(width), held(kv_all)],
            scratch_shapes=[
                pltpu.VMEM((2, 2 * tall, LANES), BF16),
                pltpu.VMEM((2, 1, tall), F32),
                pltpu.VMEM((2, tall, LANES), F32),
                pltpu.VMEM((2 * n_pairs, n_slots * rows, LANES), F32),
            ],
        ),
        name="attend_back",
    )(meta, qkv, do, o, kv_all, linv, row_pos, col_pos, cosine, sine)


def shards(
    hidden_in,
    pair_order,
    attn_gain,
    w_query,
    key_weight_matrix,
    value_weight_matrix,
    w_out,
    mlp_gain,
    w_gate,
    w_up,
    w_down,
    out_grad,
):
    n_ctx, n_fsdp = lax.axis_size(CTX), lax.axis_size(FSDP)
    my_ctx, my_fsdp = lax.axis_index(CTX), lax.axis_index(FSDP)
    resident_rows, model_width = hidden_in.shape
    half_rows = resident_rows // 2
    span = half_rows * n_fsdp
    plane_rows = resident_rows * n_ctx
    heads = QUERY_HEADS // n_ctx
    sharers = max(1, n_ctx // KEY_VALUE_HEADS)
    query_width = heads * HEAD_SIZE
    qkv_width = query_width + 2 * HEAD_SIZE
    hidden_units = w_gate.shape[1]
    unit_slice = hidden_units // n_fsdp
    weight_rows = w_gate.shape[0]

    labels = jnp.arange(n_ctx, dtype=jnp.int32)
    slot_device = my_ctx ^ jnp.array(xor_slots(n_ctx), jnp.int32)
    slot_pair = jnp.sum(
        jnp.where(slot_device[:, None] == labels[None, :], pair_order[None, :], 0), axis=1
    )
    slot_blocks = jnp.stack([slot_pair, 2 * n_ctx - 1 - slot_pair], axis=1)
    blocks = jnp.arange(2 * n_ctx, dtype=jnp.int32)
    place_of = jnp.sum(
        jnp.where(slot_blocks.reshape(-1)[None, :] == blocks[:, None], blocks[None, :], 0), axis=1
    )
    meta = jnp.concatenate([slot_pair, place_of]).astype(jnp.int32)
    in_half = jnp.arange(half_rows, dtype=jnp.int32)
    my_pos = my_fsdp * half_rows + in_half
    positions = (slot_blocks[:, :, None] * span + my_pos).reshape(plane_rows)
    cosine, sine = rotate_tables(positions)
    slot_owner = (my_fsdp - jnp.arange(n_fsdp, dtype=jnp.int32)) % n_fsdp
    key_pos = (slot_owner[:, None] * half_rows + in_half[None, :]).reshape(span)
    query_pos = jnp.tile(my_pos, heads)
    as_rows = lambda v: jnp.broadcast_to(v[:, None], v.shape + (LANES,))
    as_columns = lambda v: jnp.broadcast_to(v[None, :], (8,) + v.shape)

    padded_rows = weight_rows + 8
    kv_of = lambda w: jnp.repeat(
        w.reshape(weight_rows, -1, HEAD_SIZE).transpose(1, 0, 2), sharers, axis=0
    )
    w_first = jnp.concatenate(
        [
            w_query.reshape(weight_rows, n_ctx, query_width).transpose(1, 0, 2),
            kv_of(key_weight_matrix),
            kv_of(value_weight_matrix),
        ],
        axis=2,
    )
    both_gains = jnp.concatenate([attn_gain, mlp_gain])
    gain_block = jnp.pad(both_gains[None, :], ((0, 7), (0, qkv_width - 2 * weight_rows)))
    w_first = jnp.concatenate(
        [w_first, jnp.broadcast_to(gain_block, (n_ctx,) + gain_block.shape)], axis=1
    )
    w_first = lax.all_to_all(w_first, CTX, 0, 0, tiled=True)
    w_first = lax.all_gather(w_first, FSDP, axis=1, tiled=True)
    w_first = w_first.reshape(n_ctx, n_fsdp, padded_rows, qkv_width)
    all_gains = w_first[:, :, weight_rows, : 2 * weight_rows].astype(F32)
    gain_one = all_gains[:, :, :weight_rows].reshape(1, model_width)
    gain_two = all_gains[:, :, weight_rows:].reshape(1, model_width)

    hidden_all = xor_gather(hidden_in).reshape(plane_rows, model_width)
    normed_one, qkv, w_qkv = project(
        hidden_all, gain_one, w_first, cosine, sine, query_width, weight_rows
    )
    qkv4 = qkv.reshape(n_ctx, 2, half_rows, qkv_width)
    kv_all = z_gather(qkv[:, query_width:])
    kv_all = kv_all.reshape(n_fsdp, n_ctx, 2, half_rows, LANES)


    def by_slice(w):
        return w.reshape(weight_rows, n_fsdp, unit_slice).transpose(1, 0, 2)

    def exchange_two(a, b, *others):
        both = jnp.concatenate([a, b], axis=2)
        both = z_exchange(after(both, *others))
        return both[..., : a.shape[2]], both[..., a.shape[2] :]

    def whole(mine):
        return ctx_gather(mine.reshape(n_fsdp * weight_rows, -1))

    w_out_slice = z_spread(lambda d: w_out).reshape(-1, model_width)
    gate_mine = z_spread(lambda d: lax.dynamic_slice_in_dim(w_gate, d * unit_slice, unit_slice, 1))
    gate_w = whole(gate_mine)
    up_mine, down_mine = exchange_two(by_slice(w_up), by_slice(w_down.T), kv_all)
    up_w, down_t = whole(up_mine), whole(down_mine)
    grad_all = z_gather(after(out_grad, up_mine))

    o_full, o_b, linv = attend(
        meta, qkv4, after(kv_all, gate_mine), as_rows(query_pos), as_columns(key_pos), heads
    )
    o_b = o_b.reshape(plane_rows, query_width)
    residual = hidden_in.astype(F32)
    out_product = mm(o_b, w_out_slice, NN, BF16)
    attn_out = xor_reduce(out_product.reshape(n_ctx, resident_rows, -1))
    after_attn = residual + attn_out
    scale_two = lax.rsqrt(jnp.mean(after_attn * after_attn, axis=1, keepdims=True) + norm_eps)
    unit_two = after_attn * scale_two
    normed_two = z_gather((unit_two * gain_two).astype(BF16))

    gate_proj = mm(normed_two, gate_w)
    up_proj = mm(normed_two, up_w)
    gate_proj, up_proj = lax.optimization_barrier((gate_proj, up_proj))
    d_act = mm(grad_all, down_t)
    sigmoid_gate = jax.nn.sigmoid(gate_proj)
    activated = (gate_proj * sigmoid_gate * up_proj).astype(BF16)
    d_gate = (d_act * up_proj * sigmoid_gate * (1.0 + gate_proj * (1.0 - sigmoid_gate))).astype(
        BF16
    )
    d_up = (d_act * gate_proj * sigmoid_gate).astype(BF16)
    d_normed_partial = (mm(d_gate, gate_w, NT) + mm(d_up, up_w, NT)).astype(BF16)
    d_normed_two = z_reduce(d_normed_partial)

    ffn_partials = [
        mm(after(grad_all, d_normed_partial), activated, TN, BF16),
        mm(after(normed_two, d_normed_partial), d_gate, TN, BF16),
        mm(after(normed_two, d_normed_partial), d_up, TN, BF16),
    ]
    ffn_grads = [ctx_reduce(g) for g in ffn_partials]
    result_partial = mm(after(activated, d_normed_two), down_t, NT, BF16)
    result = after_attn + z_reduce(after(result_partial, d_normed_two))

    gain_two_grad = jnp.sum(d_normed_two * unit_two, axis=0)
    d_unit_two = d_normed_two * gain_two
    d_mixed = out_grad.astype(F32) + scale_two * (
        d_unit_two - unit_two * jnp.mean(d_unit_two * unit_two, axis=1, keepdims=True)
    )
    d_attn = xor_gather(d_mixed.astype(BF16)).reshape(plane_rows, model_width)
    d_attn = after(d_attn, *ffn_partials)
    d_o = mm(d_attn, w_out_slice, NT, BF16)
    out_partial = mm(o_b, d_attn, TN, BF16).reshape(n_fsdp, weight_rows, model_width)
    grad_out_w = z_sum(lambda d: lax.dynamic_index_in_dim(out_partial, d, 0, False))
    pair_view = lambda x: x.reshape(n_ctx, 2, half_rows, -1)
    dq, dkv_all = attend_back(
        meta,
        qkv4,
        pair_view(d_o),
        o_full,
        kv_all,
        linv,
        as_rows(key_pos),
        as_columns(query_pos),
        pair_view(cosine),
        pair_view(sine),
        heads,
    )
    dkv = z_reduce(dkv_all.reshape(n_fsdp * plane_rows, LANES))
    dkv = unrotate(dkv, cosine, sine)
    d_qkv = jnp.concatenate([dq.reshape(plane_rows, query_width), dkv], axis=1)
    d_first_partial = mm(d_qkv, w_qkv, NT, BF16)
    d_normed_one = xor_reduce(d_first_partial.reshape(n_ctx, resident_rows, -1))

    scale_one = lax.rsqrt(jnp.mean(residual * residual, axis=1, keepdims=True) + norm_eps)
    unit_one = residual * scale_one
    d_unit_one = d_normed_one * gain_one
    grad_in = d_mixed + scale_one * (
        d_unit_one - unit_one * jnp.mean(d_unit_one * unit_one, axis=1, keepdims=True)
    )

    wide = hidden_all.astype(F32)
    scale_all = lax.rsqrt(jnp.mean(wide * wide, axis=1, keepdims=True) + norm_eps)
    gain_one_grad = jnp.sum(d_first_partial.astype(F32) * (wide * scale_all), axis=0)
    by_owner = lambda g: g.reshape(n_ctx, n_fsdp, weight_rows)
    gain_grads = jnp.concatenate([by_owner(gain_one_grad), by_owner(gain_two_grad)], axis=2)
    gain_grads = jnp.pad(
        gain_grads[:, :, None, :].astype(BF16),
        ((0, 0), (0, 0), (0, 7), (0, qkv_width - 2 * weight_rows)),
    )
    first_grads = mm(normed_one, d_qkv, TN, BF16).reshape(n_ctx, n_fsdp, weight_rows, qkv_width)
    first_grads = jnp.concatenate(
        [first_grads.transpose(1, 0, 2, 3), gain_grads.transpose(1, 0, 2, 3)], axis=2
    )
    first_sum = jnp.sum(z_exchange(first_grads).astype(F32), axis=0)
    first_home = lax.all_to_all(first_sum.astype(BF16), CTX, 0, 0, tiled=True).astype(F32)

    def part_home(start, width, share):
        part = first_home[:, :weight_rows, start : start + width]
        part = jnp.sum(part.reshape(n_ctx // share, share, weight_rows, width), axis=1)
        return part.transpose(1, 0, 2).reshape(weight_rows, -1)

    query_sum = part_home(0, query_width, 1)
    key_sum = part_home(query_width, HEAD_SIZE, sharers)
    value_sum = part_home(query_width + HEAD_SIZE, HEAD_SIZE, sharers)
    gain_sums = jnp.sum(first_home[:, weight_rows, : 2 * weight_rows], axis=0)

    def columns_home(pieces):
        return pieces.transpose(1, 0, 2).reshape(weight_rows, hidden_units).astype(F32)

    homes = [g.reshape(n_fsdp, weight_rows, unit_slice) for g in ffn_grads]
    down_sum = columns_home(z_exchange(homes[0]))
    gate_sum = columns_home(z_exchange(homes[1]))
    up_pick = lambda d: lax.dynamic_index_in_dim(homes[2], d, 0, False)
    up_sum = columns_home(z_spread(up_pick))
    return (
        result,
        grad_in,
        gain_sums[:weight_rows],
        query_sum,
        key_sum,
        value_sum,
        grad_out_w,
        gain_sums[weight_rows:],
        gate_sum,
        up_sum,
        down_sum.T,
    )


def solution(mesh):
    rows, columns, vector = P(BOTH, None), P(None, BOTH), P(BOTH)
    placed = (rows, P(), vector, rows, rows, rows, rows, vector, rows, rows, columns, rows)

    return jax.shard_map(
        shards,
        mesh=mesh,
        in_specs=placed,
        out_specs=(rows, rows, vector, rows, rows, rows, rows, vector, rows, rows, columns),
        check_vma=False,
    )
```

```python
import functools

import jax
import jax.numpy as jnp
from jax import lax
from jax.experimental import pallas as pl
from jax.experimental.pallas import tpu as pltpu
from jax.sharding import PartitionSpec as P


QUERY_HEADS = 32
KEY_VALUE_HEADS = 8
HEAD_SIZE = 64
LANES = 128

rope_base = 500000.0
norm_eps = 1e-05
CTX, FSDP = BOTH = ("ctx", "fsdp")
BF16, F32 = jnp.bfloat16, jnp.float32


NT = (((1,), (1,)), ((), ()))
TN = (((0,), (0,)), ((), ()))
NN = (((1,), (0,)), ((), ()))


def mm(a, b, dims=NN, out=F32):
    return lax.dot_general(a, b, dims, preferred_element_type=F32).astype(out)


def shift_perm(n, s):
    return [(i, (i + s) % n) for i in range(n)]


def z_gather(x):
    n = lax.axis_size(FSDP)
    parts = [x] + [lax.ppermute(x, FSDP, shift_perm(n, s)) for s in range(1, n)]
    return jnp.concatenate(parts, axis=0)


def z_reduce(partial):
    n = lax.axis_size(FSDP)
    rows = partial.shape[0] // n
    total = partial[:rows].astype(F32)
    for s in range(1, n):
        piece = partial[s * rows : (s + 1) * rows].astype(BF16)
        total = total + lax.ppermute(piece, FSDP, shift_perm(n, -s)).astype(F32)
    return total


def z_exchange(x):
    return lax.all_to_all(x, FSDP, 0, 0, tiled=True)


def z_sum(pick):
    n, me = lax.axis_size(FSDP), lax.axis_index(FSDP)
    total = pick(me).astype(F32)
    for s in range(1, n):
        got = lax.ppermute(pick((me + s) % n), FSDP, shift_perm(n, s))
        total = total + got.astype(F32)
    return total


def z_spread(pick):
    n, me = lax.axis_size(FSDP), lax.axis_index(FSDP)
    own = pick(me)
    out = jnp.zeros((n,) + own.shape, own.dtype)
    out = lax.dynamic_update_index_in_dim(out, own, me, 0)
    for s in range(1, n):
        got = lax.ppermute(pick((me + s) % n), FSDP, shift_perm(n, s))
        out = lax.dynamic_update_index_in_dim(out, got, (me - s) % n, 0)
    return out


def ctx_gather(x):
    return lax.all_gather(x, CTX, axis=0, tiled=True)


def chip_reduce(x):
    n = lax.axis_size(CTX)
    groups = [list(range(core, n, 2)) for core in range(2)]
    return lax.psum_scatter(
        x, CTX, scatter_dimension=0, axis_index_groups=groups, tiled=True
    )


def xor_slots(n):
    return list(range(0, n, 2)) + list(range(1, n, 2))


def xor_swap(x, bit):
    n = lax.axis_size(CTX)
    return lax.ppermute(x, CTX, [(i, i ^ bit) for i in range(n)])


def bit_orders(n):
    bits = [1 << b for b in range(1, n.bit_length() - 1)]
    return bits, bits[::-1]


def xor_gather(x):
    n, rows = lax.axis_size(CTX), x.shape[0] // 2
    halves = []
    for order, piece in zip(bit_orders(n), (x[:rows], x[rows:])):
        parts = {0: piece}
        for bit in order:
            parts.update({m ^ bit: xor_swap(part, bit) for m, part in list(parts.items())})
        halves.append(parts)
    mine = jnp.stack(
        [jnp.concatenate([half[m] for half in halves], axis=0) for m in xor_slots(n)[: n // 2]]
    )
    flat = lambda y: y.reshape(-1, x.shape[1])
    return flat(mine), flat(xor_swap(mine, 1))


def xor_reduce(x):
    n, rows = lax.axis_size(CTX), x.shape[1] // 2
    got = xor_swap(x[n // 2 :], 1)
    mine = (x[: n // 2].astype(F32) + got.astype(F32)).astype(BF16)
    done = []
    for order, cut in zip(bit_orders(n), (slice(None, rows), slice(rows, None))):
        parts = {m: mine[i, cut] for i, m in enumerate(xor_slots(n)[: n // 2])}
        for bit in order:
            away = sorted(m for m in parts if m & bit)
            got = xor_swap(jnp.stack([parts[m] for m in away]), bit)
            for i, m in enumerate(away):
                kept = parts[m ^ bit].astype(F32) + got[i].astype(F32)
                parts[m ^ bit] = kept if len(away) == 1 else kept.astype(BF16)
                del parts[m]
        done.append(parts[0])
    return jnp.concatenate(done, axis=0)


def after(x, *others):
    return lax.optimization_barrier((x,) + others)[0]


def rotate_tile(x, cosine, sine):
    lane = lax.broadcasted_iota(jnp.int32, x.shape, 1)
    low = (lane % HEAD_SIZE) < HEAD_SIZE // 2
    width = x.shape[1]
    swapped = jnp.where(
        low, pltpu.roll(x, width - HEAD_SIZE // 2, 1), pltpu.roll(x, HEAD_SIZE // 2, 1)
    )
    return x * cosine + swapped * sine


def rotate_tables(positions):
    lane = jnp.arange(LANES, dtype=jnp.int32)
    frequency = 1.0 / rope_base ** (
        jnp.arange(0, HEAD_SIZE, 2, dtype=F32) / HEAD_SIZE
    )
    frequency = jnp.tile(frequency, LANES // (HEAD_SIZE // 2))
    angles = positions.astype(F32)[:, None] * frequency[None, :]
    sign = jnp.where((lane % HEAD_SIZE) < HEAD_SIZE // 2, -1.0, 1.0)
    return jnp.cos(angles), jnp.sin(angles) * sign[None, :]


def project_body(
    x_ref, gain_ref, w_ref, cos_ref, sin_ref, normed_ref, out_ref, flat_ref, *, query_width, rows
):
    @pl.when(pl.program_id(0) == 0)
    def _():
        flat_ref[...] = w_ref[:, :, :rows, :].reshape(flat_ref.shape)

    x = x_ref[...].astype(F32)
    scale = lax.rsqrt(jnp.mean(x * x, axis=1, keepdims=True) + norm_eps)
    normed = (x * scale * gain_ref[...]).astype(BF16)
    normed_ref[...] = normed
    tile = jnp.dot(normed, flat_ref[...], preferred_element_type=F32)
    for i in range(out_ref.shape[1] // LANES):
        part = tile[:, i * LANES : (i + 1) * LANES]
        column = i * LANES + lax.broadcasted_iota(jnp.int32, part.shape, 1)
        turned = rotate_tile(part, cos_ref[...], sin_ref[...])
        part = jnp.where(column < query_width + HEAD_SIZE, turned, part)
        scale = jnp.where(column < query_width, HEAD_SIZE ** (-0.5), 1.0)
        out_ref[:, i * LANES : (i + 1) * LANES] = (part * scale).astype(BF16)


def project(x, gain, w, cosine, sine, query_width, w_rows):
    rows, depth = x.shape
    width = w.shape[3]
    tile = min(rows, 256)
    return pl.pallas_call(
        functools.partial(project_body, query_width=query_width, rows=w_rows),
        out_shape=(
            jax.ShapeDtypeStruct((rows, depth), BF16),
            jax.ShapeDtypeStruct((rows, width), BF16),
            jax.ShapeDtypeStruct((depth, width), BF16),
        ),
        grid=(rows // tile,),
        in_specs=[
            pl.BlockSpec((tile, depth), lambda i: (i, 0)),
            pl.BlockSpec((1, depth), lambda i: (0, 0)),
            pl.BlockSpec(w.shape, lambda i: (0, 0, 0, 0)),
            pl.BlockSpec((tile, LANES), lambda i: (i, 0)),
            pl.BlockSpec((tile, LANES), lambda i: (i, 0)),
        ],
        out_specs=[
            pl.BlockSpec((tile, depth), lambda i: (i, 0)),
            pl.BlockSpec((tile, width), lambda i: (i, 0)),
            pl.BlockSpec((depth, width), lambda i: (0, 0)),
        ],
        name="project",
    )(x, gain, w, cosine, sine)


def unrotate_body(x_ref, cos_ref, sin_ref, out_ref):
    part = x_ref[...]
    lane = lax.broadcasted_iota(jnp.int32, part.shape, 1)
    turned = rotate_tile(part, cos_ref[...], -sin_ref[...])
    out_ref[...] = jnp.where(lane < HEAD_SIZE, turned, part).astype(BF16)


def unrotate(x, cosine, sine):
    return pl.pallas_call(
        unrotate_body, out_shape=jax.ShapeDtypeStruct(x.shape, BF16), name="unrotate"
    )(x, cosine, sine)


def stack_heads(x, heads, high):
    out = []
    for h in range(heads):
        tile = x[:, (h // 2) * LANES : (h // 2 + 1) * LANES].astype(F32)
        if (h % 2 == 1) != high:
            tile = pltpu.roll(tile, HEAD_SIZE, 1)
        lane = lax.broadcasted_iota(jnp.int32, tile.shape, 1)
        out.append(jnp.where((lane >= HEAD_SIZE) == high, tile, 0.0))
    return jnp.concatenate(out, axis=0)


def join_heads(stacked, heads, high):
    rows = stacked.shape[0] // heads
    for pair in range(heads // 2):
        even = stacked[2 * pair * rows : (2 * pair + 1) * rows]
        odd = stacked[(2 * pair + 1) * rows : (2 * pair + 2) * rows]
        if high:
            even = pltpu.roll(even, HEAD_SIZE, 1)
        else:
            odd = pltpu.roll(odd, HEAD_SIZE, 1)
        lane = lax.broadcasted_iota(jnp.int32, even.shape, 1)
        yield slice(pair * LANES, (pair + 1) * LANES), jnp.where(lane < HEAD_SIZE, even, odd)


def lane_sums(e):
    total = e[:, :LANES]
    for i in range(1, e.shape[1] // LANES):
        total = total + e[:, i * LANES : (i + 1) * LANES]
    return total


def across(x):
    return jnp.sum(x.T, axis=0, keepdims=True)


def items(meta, step, n_blocks):
    early = meta[step]
    place = lambda block: meta[n_blocks // 2 + block]
    for half in range(2):
        yield half, place(early if half == 0 else n_blocks - 1 - early), True
    for t in range(n_blocks - 1):
        late = t >= early
        yield late.astype(jnp.int32), place(jnp.where(late, t - early, t)), False


def attend_body(
    meta, q_ref, kv_ref, row_ref, col_ref, o_ref, ob_ref, linv_ref, qs_ref, acc_ref, l_ref, *, heads
):
    step = pl.program_id(0)
    n_slots, n_pairs, _, rows, _ = kv_ref.shape
    for half in range(2):
        qs_ref[half] = stack_heads(q_ref[0, half], heads, False).astype(BF16)
    acc_ref[...] = jnp.zeros_like(acc_ref)
    l_ref[...] = jnp.zeros_like(l_ref)

    def scores(half, place, diagonal):
        kv = kv_ref[:, place // 2, place % 2].reshape(n_slots * rows, LANES)
        return half, diagonal, kv, lax.dot_general(qs_ref[half], kv, NT, preferred_element_type=F32)

    def weigh(half, diagonal, kv, s):
        e = jnp.exp(s)
        if diagonal:
            e = jnp.where(col_ref[0:1, :] <= row_ref[:, 0:1], e, 0.0)
        l_ref[half] += lane_sums(e)
        acc_ref[half] += jnp.dot(e.astype(BF16), kv, preferred_element_type=F32)

    ahead = None
    for item in items(meta, step, 2 * n_pairs):
        now, ahead = ahead, scores(*item)
        if now is not None:
            weigh(*now)
    weigh(*ahead)
    for half in range(2):
        sums = l_ref[half]
        linv_ref[0, half : half + 1, :] = 1.0 / across(sums)
        out = acc_ref[half] * (1.0 / jnp.sum(sums, axis=1, keepdims=True))
        for columns, tile in join_heads(out, heads, True):
            o_ref[0, half, :, columns] = tile
            ob_ref[0, half, :, columns] = tile.astype(BF16)


def attend_back_body(
    meta, q_ref, do_ref, o_ref, kv_ref, linv_ref, row_ref, col_ref, cos_ref, sin_ref,
    dq_ref, dkv_ref, qd_ref, delta_ref, dq_acc, dkv_acc, *, heads
):
    step = pl.program_id(0)
    n_slots, n_pairs, _, rows, _ = kv_ref.shape
    span, tall = n_slots * rows, heads * rows

    @pl.when(step == 0)
    def _():
        dkv_acc[...] = jnp.zeros_like(dkv_acc)

    dq_acc[...] = jnp.zeros_like(dq_acc)
    for half in range(2):
        qd_ref[half, :tall] = stack_heads(q_ref[0, half], heads, False).astype(BF16)
        do = stack_heads(do_ref[0, half], heads, True)
        qd_ref[half, tall:] = do.astype(BF16)
        delta_ref[half] = across(do * stack_heads(o_ref[0, half], heads, True))

    def scores(half, place, diagonal):
        kv = kv_ref[:, place // 2, place % 2].reshape(span, LANES)
        s = lax.dot_general(kv, qd_ref[half, :tall], NT, preferred_element_type=F32)
        dp = lax.dot_general(kv, qd_ref[half, tall:], NT, preferred_element_type=F32)
        return half, place, diagonal, kv, s, dp

    def gradients(half, place, diagonal, kv, s, dp):
        p = jnp.exp(s) * linv_ref[0, pl.ds(half, 1), :]
        if diagonal:
            p = jnp.where(row_ref[:, 0:1] <= col_ref[0:1, :], p, 0.0)
        ds = (p * (dp - delta_ref[half])).astype(BF16)
        dkv_acc[place] += jnp.dot(
            jnp.concatenate([ds, p.astype(BF16)], axis=1), qd_ref[half], preferred_element_type=F32
        )
        dq_acc[half] += lax.dot_general(ds, kv, TN, preferred_element_type=F32)

    ahead = None
    for item in items(meta, step, 2 * n_pairs):
        now, ahead = ahead, scores(*item)
        if now is not None:
            gradients(*now)
    gradients(*ahead)
    for half in range(2):
        for columns, tile in join_heads(dq_acc[half] * HEAD_SIZE ** (-0.5), heads, False):
            turned = rotate_tile(tile, cos_ref[0, half], -sin_ref[0, half])
            dq_ref[0, half, :, columns] = turned.astype(BF16)

    @pl.when(step == pl.num_programs(0) - 1)
    def _():
        for place in range(2 * n_pairs):
            dkv_ref[:, place // 2, place % 2] = (
                dkv_acc[place].astype(BF16).reshape(n_slots, rows, LANES)
            )


def attention_specs(kv_all):
    _, _, _, rows, _ = kv_all.shape
    pair = lambda w: pl.BlockSpec((1, 2, rows, w), lambda j, m: (j, 0, 0, 0))
    held = lambda x: pl.BlockSpec(x.shape, lambda j, m: (0,) * len(x.shape))
    return pair, held


def attend(meta, qkv, kv_all, row_pos, col_pos, heads):
    _, n_pairs, _, rows, _ = kv_all.shape
    width = heads * HEAD_SIZE
    pair, held = attention_specs(kv_all)
    across_spec = pl.BlockSpec((1, 2, heads * rows), lambda j, m: (j, 0, 0))
    return pl.pallas_call(
        functools.partial(attend_body, heads=heads),
        out_shape=(
            jax.ShapeDtypeStruct((n_pairs, 2, rows, width), F32),
            jax.ShapeDtypeStruct((n_pairs, 2, rows, width), BF16),
            jax.ShapeDtypeStruct((n_pairs, 2, heads * rows), F32),
        ),
        grid_spec=pltpu.PrefetchScalarGridSpec(
            num_scalar_prefetch=1,
            grid=(n_pairs,),
            in_specs=[pair(width), held(kv_all), held(row_pos), held(col_pos)],
            out_specs=[pair(width), pair(width), across_spec],
            scratch_shapes=[
                pltpu.VMEM((2, heads * rows, LANES), BF16),
                pltpu.VMEM((2, heads * rows, LANES), F32),
                pltpu.VMEM((2, heads * rows, LANES), F32),
            ],
        ),
        name="attend",
    )(meta, qkv, kv_all, row_pos, col_pos)


def attend_back(meta, qkv, do, o, kv_all, linv, row_pos, col_pos, cosine, sine, heads):
    n_slots, n_pairs, _, rows, _ = kv_all.shape
    width, tall = heads * HEAD_SIZE, heads * rows
    pair, held = attention_specs(kv_all)
    across_spec = pl.BlockSpec((1, 2, tall), lambda j, m: (j, 0, 0))
    return pl.pallas_call(
        functools.partial(attend_back_body, heads=heads),
        out_shape=(
            jax.ShapeDtypeStruct((n_pairs, 2, rows, width), BF16),
            jax.ShapeDtypeStruct(kv_all.shape, BF16),
        ),
        grid_spec=pltpu.PrefetchScalarGridSpec(
            num_scalar_prefetch=1,
            grid=(n_pairs,),
            in_specs=[
                pair(width), pair(width), pair(width), held(kv_all), across_spec,
                held(row_pos), held(col_pos), pair(LANES), pair(LANES),
            ],
            out_specs=[pair(width), held(kv_all)],
            scratch_shapes=[
                pltpu.VMEM((2, 2 * tall, LANES), BF16),
                pltpu.VMEM((2, 1, tall), F32),
                pltpu.VMEM((2, tall, LANES), F32),
                pltpu.VMEM((2 * n_pairs, n_slots * rows, LANES), F32),
            ],
        ),
        name="attend_back",
    )(meta, qkv, do, o, kv_all, linv, row_pos, col_pos, cosine, sine)


def hidden_back_body(
    dy_ref, gate_ref, up_ref, down_ref, wg_ref, wu_ref, act_ref, dg_ref, du_ref, dn_ref, da_ref,
    acc_ref,
):
    step = pl.program_id(0)
    rows, width = acc_ref.shape
    da_ref[...] = jnp.dot(dy_ref[...], down_ref[...], preferred_element_type=F32)

    @pl.when(step == 0)
    def _():
        acc_ref[...] = jnp.zeros_like(acc_ref)

    few = min(rows, 64)
    for r in range(0, rows, few):
        cut = slice(r, r + few)
        gate, up, d_act = gate_ref[cut], up_ref[cut], da_ref[cut]
        sigma = 1.0 / (1.0 + jnp.exp(-gate))
        act_ref[cut] = (gate * sigma * up).astype(BF16)
        dg_ref[cut] = (d_act * up * sigma * (1.0 + gate * (1.0 - sigma))).astype(BF16)
        du_ref[cut] = (d_act * gate * sigma).astype(BF16)
    some = min(width, 256)
    for c in range(0, width, some):
        cut = slice(c, c + some)
        part = lax.dot_general(dg_ref[...], wg_ref[cut], NT, preferred_element_type=F32)
        part = part + lax.dot_general(du_ref[...], wu_ref[cut], NT, preferred_element_type=F32)
        acc_ref[:, cut] += part

    @pl.when(step == pl.num_programs(0) - 1)
    def _():
        dn_ref[...] = acc_ref[...].astype(BF16)


def hidden_back(dy, gate, up, down_t, gate_w, up_w):
    rows, width = dy.shape
    units = gate.shape[1]
    tile = min(units, 256)
    held = pl.BlockSpec((rows, width), lambda i: (0, 0))
    tall = pl.BlockSpec((width, tile), lambda i: (0, i))
    part = pl.BlockSpec((rows, tile), lambda i: (0, i))
    return pl.pallas_call(
        hidden_back_body,
        out_shape=(jax.ShapeDtypeStruct((rows, units), BF16),) * 3
        + (jax.ShapeDtypeStruct((rows, width), BF16),),
        grid=(units // tile,),
        in_specs=[held, part, part, tall, tall, tall],
        out_specs=[part, part, part, held],
        scratch_shapes=[pltpu.VMEM((rows, tile), F32), pltpu.VMEM((rows, width), F32)],
        name="hidden_back",
    )(dy, gate, up, down_t, gate_w, up_w)


def core_rows_body(core, x_ref, y_ref, *refs):
    del core
    total = lax.dot_general(x_ref[...], y_ref[...], TN, preferred_element_type=F32)
    for ref in refs[:-1]:
        total = total + ref[...].astype(F32)
    refs[-1][...] = total.astype(BF16)


def core_rows(core, x, y, block, *addends):
    rows, depth = x.shape
    width = y.shape[1]
    n_chips = depth // block // 2
    out = pl.BlockSpec((block, width), lambda i, k: (i, 0))
    return pl.pallas_call(
        core_rows_body,
        out_shape=jax.ShapeDtypeStruct((n_chips * block, width), BF16),
        grid_spec=pltpu.PrefetchScalarGridSpec(
            num_scalar_prefetch=1,
            grid=(n_chips,),
            in_specs=[
                pl.BlockSpec((rows, block), lambda i, k: (0, 2 * i + k[0])),
                pl.BlockSpec((rows, width), lambda i, k: (0, 0)),
            ]
            + [out] * len(addends),
            out_specs=out,
        ),
        name="core_rows",
    )(core, x, y, *addends)


def shards(
    hidden_in,
    pair_order,
    attn_gain,
    w_query,
    key_weight_matrix,
    value_weight_matrix,
    w_out,
    mlp_gain,
    w_gate,
    w_up,
    w_down,
    out_grad,
):
    n_ctx, n_fsdp = lax.axis_size(CTX), lax.axis_size(FSDP)
    my_ctx, my_fsdp = lax.axis_index(CTX), lax.axis_index(FSDP)
    resident_rows, model_width = hidden_in.shape
    half_rows = resident_rows // 2
    span = half_rows * n_fsdp
    plane_rows = resident_rows * n_ctx
    heads = QUERY_HEADS // n_ctx
    sharers = max(1, n_ctx // KEY_VALUE_HEADS)
    query_width = heads * HEAD_SIZE
    qkv_width = query_width + 2 * HEAD_SIZE
    hidden_units = w_gate.shape[1]
    unit_slice = hidden_units // n_fsdp
    weight_rows = w_gate.shape[0]

    labels = jnp.arange(n_ctx, dtype=jnp.int32)
    slot_device = my_ctx ^ jnp.array(xor_slots(n_ctx), jnp.int32)
    slot_pair = jnp.sum(
        jnp.where(slot_device[:, None] == labels[None, :], pair_order[None, :], 0), axis=1
    )
    slot_blocks = jnp.stack([slot_pair, 2 * n_ctx - 1 - slot_pair], axis=1)
    blocks = jnp.arange(2 * n_ctx, dtype=jnp.int32)
    place_of = jnp.sum(
        jnp.where(slot_blocks.reshape(-1)[None, :] == blocks[:, None], blocks[None, :], 0), axis=1
    )
    meta = jnp.concatenate([slot_pair, place_of]).astype(jnp.int32)
    in_half = jnp.arange(half_rows, dtype=jnp.int32)
    my_pos = my_fsdp * half_rows + in_half
    positions = (slot_blocks[:, :, None] * span + my_pos).reshape(plane_rows)
    cosine, sine = lax.optimization_barrier(rotate_tables(positions))
    slot_owner = (my_fsdp - jnp.arange(n_fsdp, dtype=jnp.int32)) % n_fsdp
    key_pos = (slot_owner[:, None] * half_rows + in_half[None, :]).reshape(span)
    query_pos = jnp.tile(my_pos, heads)
    as_rows = lambda v: jnp.broadcast_to(v[:, None], v.shape + (LANES,))
    as_columns = lambda v: jnp.broadcast_to(v[None, :], (8,) + v.shape)

    padded_rows = weight_rows + 8
    kv_of = lambda w: jnp.repeat(
        w.reshape(weight_rows, -1, HEAD_SIZE).transpose(1, 0, 2), sharers, axis=0
    )
    w_first = jnp.concatenate(
        [
            w_query.reshape(weight_rows, n_ctx, query_width).transpose(1, 0, 2),
            kv_of(key_weight_matrix),
            kv_of(value_weight_matrix),
        ],
        axis=2,
    )
    both_gains = jnp.concatenate([attn_gain, mlp_gain])
    gain_block = jnp.pad(both_gains[None, :], ((0, 7), (0, qkv_width - 2 * weight_rows)))
    w_first = jnp.concatenate(
        [w_first, jnp.broadcast_to(gain_block, (n_ctx,) + gain_block.shape)], axis=1
    )
    w_first = lax.all_to_all(w_first, CTX, 0, 0, tiled=True)
    w_first = lax.all_gather(w_first, FSDP, axis=1, tiled=True)
    w_first = w_first.reshape(n_ctx, n_fsdp, padded_rows, qkv_width)
    all_gains = w_first[:, :, weight_rows, : 2 * weight_rows].astype(F32)
    gain_one = all_gains[:, :, :weight_rows].reshape(1, model_width)
    gain_two = all_gains[:, :, weight_rows:].reshape(1, model_width)

    hidden_all = jnp.concatenate(xor_gather(hidden_in), axis=0)
    normed_one, qkv, w_qkv = project(
        hidden_all, gain_one, w_first, cosine, sine, query_width, weight_rows
    )
    qkv4 = qkv.reshape(n_ctx, 2, half_rows, qkv_width)
    kv_all = z_gather(qkv[:, query_width:])
    kv_all = kv_all.reshape(n_fsdp, n_ctx, 2, half_rows, LANES)


    def by_slice(w):
        return w.reshape(weight_rows, n_fsdp, unit_slice).transpose(1, 0, 2)

    def exchange_two(a, b, *others):
        both = jnp.concatenate([a, b], axis=2)
        both = z_exchange(after(both, *others))
        return both[..., : a.shape[2]], both[..., a.shape[2] :]

    def whole(mine):
        return ctx_gather(mine.reshape(n_fsdp * weight_rows, -1))

    w_out_slice = z_spread(lambda d: w_out).reshape(-1, model_width)
    gate_mine = z_spread(lambda d: lax.dynamic_slice_in_dim(w_gate, d * unit_slice, unit_slice, 1))
    gate_w = whole(gate_mine)
    up_mine, down_mine = exchange_two(by_slice(w_up), by_slice(w_down.T), kv_all)
    up_w, down_t = whole(up_mine), whole(down_mine)
    grad_all = z_gather(after(out_grad, up_mine))

    o_full, o_b, linv = attend(
        meta, qkv4, after(kv_all, gate_mine), as_rows(query_pos), as_columns(key_pos), heads
    )
    o_b = o_b.reshape(plane_rows, query_width)
    residual = hidden_in.astype(F32)
    out_product = mm(o_b, w_out_slice, NN, BF16)
    attn_out = xor_reduce(out_product.reshape(n_ctx, resident_rows, -1))
    after_attn = residual + attn_out
    scale_two = lax.rsqrt(jnp.mean(after_attn * after_attn, axis=1, keepdims=True) + norm_eps)
    unit_two = after_attn * scale_two
    normed_two = z_gather((unit_two * gain_two).astype(BF16))

    gate_proj = mm(normed_two, gate_w)
    up_proj = mm(normed_two, up_w)
    activated, d_gate, d_up, d_normed_partial = hidden_back(
        grad_all, gate_proj, up_proj, down_t, gate_w, up_w
    )
    d_normed_two = z_reduce(d_normed_partial)

    block = n_fsdp * weight_rows
    core = (my_ctx % 2).reshape(1)
    normed_late = after(normed_two, d_normed_partial)
    factors = (
        (after(grad_all, d_normed_partial), activated),
        (normed_late, d_gate),
        (normed_late, d_up),
    )
    away = [core_rows(1 - core, x, y, block) for x, y in factors]
    got = [xor_swap(x, 1) for x in away]
    ffn_partials = [core_rows(core, x, y, block, z) for (x, y), z in zip(factors, got)]
    ffn_grads = [chip_reduce(g) for g in ffn_partials]
    result_partial = mm(after(activated, d_normed_two), down_t, NT, BF16)
    result = after_attn + z_reduce(after(result_partial, d_normed_two))

    gain_two_grad = jnp.sum(d_normed_two * unit_two, axis=0)
    d_unit_two = d_normed_two * gain_two
    d_mixed = out_grad.astype(F32) + scale_two * (
        d_unit_two - unit_two * jnp.mean(d_unit_two * unit_two, axis=1, keepdims=True)
    )
    d_mine, d_other = xor_gather(d_mixed.astype(BF16))
    d_mine = after(d_mine, *ffn_partials)
    d_o = jnp.concatenate(
        [mm(d_mine, w_out_slice, NT, BF16), mm(d_other, w_out_slice, NT, BF16)], axis=0
    )
    middle = plane_rows // 2
    out_partial = mm(o_b[:middle], d_mine, TN) + mm(o_b[middle:], d_other, TN)
    out_partial = out_partial.astype(BF16).reshape(n_fsdp, weight_rows, model_width)
    grad_out_w = z_sum(lambda d: lax.dynamic_index_in_dim(out_partial, d, 0, False))
    pair_view = lambda x: x.reshape(n_ctx, 2, half_rows, -1)
    dq, dkv_all = attend_back(
        meta,
        qkv4,
        pair_view(d_o),
        o_full,
        kv_all,
        linv,
        as_rows(key_pos),
        as_columns(query_pos),
        pair_view(cosine),
        pair_view(sine),
        heads,
    )
    dkv = z_reduce(dkv_all.reshape(n_fsdp * plane_rows, LANES))
    dkv = unrotate(dkv, cosine, sine)
    d_qkv = jnp.concatenate([dq.reshape(plane_rows, query_width), dkv], axis=1)
    d_first_partial = mm(d_qkv, w_qkv, NT, BF16)
    d_normed_one = xor_reduce(d_first_partial.reshape(n_ctx, resident_rows, -1))

    scale_one = lax.rsqrt(jnp.mean(residual * residual, axis=1, keepdims=True) + norm_eps)
    unit_one = residual * scale_one
    d_unit_one = d_normed_one * gain_one
    grad_in = d_mixed + scale_one * (
        d_unit_one - unit_one * jnp.mean(d_unit_one * unit_one, axis=1, keepdims=True)
    )

    wide = hidden_all.astype(F32)
    scale_all = lax.rsqrt(jnp.mean(wide * wide, axis=1, keepdims=True) + norm_eps)
    gain_one_grad = jnp.sum(d_first_partial.astype(F32) * (wide * scale_all), axis=0)
    by_owner = lambda g: g.reshape(n_ctx, n_fsdp, weight_rows)
    gain_grads = jnp.concatenate([by_owner(gain_one_grad), by_owner(gain_two_grad)], axis=2)
    gain_grads = jnp.pad(
        gain_grads[:, :, None, :].astype(BF16),
        ((0, 0), (0, 0), (0, 7), (0, qkv_width - 2 * weight_rows)),
    )
    first_grads = mm(normed_one, d_qkv, TN, BF16).reshape(n_ctx, n_fsdp, weight_rows, qkv_width)
    first_grads = jnp.concatenate(
        [first_grads.transpose(1, 0, 2, 3), gain_grads.transpose(1, 0, 2, 3)], axis=2
    )
    first_sum = jnp.sum(z_exchange(first_grads).astype(F32), axis=0)
    first_home = lax.all_to_all(first_sum.astype(BF16), CTX, 0, 0, tiled=True).astype(F32)

    def part_home(start, width, share):
        part = first_home[:, :weight_rows, start : start + width]
        part = jnp.sum(part.reshape(n_ctx // share, share, weight_rows, width), axis=1)
        return part.transpose(1, 0, 2).reshape(weight_rows, -1)

    query_sum = part_home(0, query_width, 1)
    key_sum = part_home(query_width, HEAD_SIZE, sharers)
    value_sum = part_home(query_width + HEAD_SIZE, HEAD_SIZE, sharers)
    gain_sums = jnp.sum(first_home[:, weight_rows, : 2 * weight_rows], axis=0)

    def columns_home(pieces):
        return pieces.transpose(1, 0, 2).reshape(weight_rows, hidden_units).astype(F32)

    homes = [g.reshape(n_fsdp, weight_rows, unit_slice) for g in ffn_grads]
    down_sum = columns_home(z_exchange(homes[0]))
    pick_of = lambda home: lambda d: lax.dynamic_index_in_dim(home, d, 0, False)
    gate_sum = columns_home(z_spread(pick_of(homes[1])))
    up_sum = columns_home(z_spread(pick_of(homes[2])))
    return (
        result,
        grad_in,
        gain_sums[:weight_rows],
        query_sum,
        key_sum,
        value_sum,
        grad_out_w,
        gain_sums[weight_rows:],
        gate_sum,
        up_sum,
        down_sum.T,
    )


def solution(mesh):
    rows, columns, vector = P(BOTH, None), P(None, BOTH), P(BOTH)
    placed = (rows, P(), vector, rows, rows, rows, rows, vector, rows, rows, columns, rows)

    return jax.shard_map(
        shards,
        mesh=mesh,
        in_specs=placed,
        out_specs=(rows, rows, vector, rows, rows, rows, rows, vector, rows, rows, columns),
        check_vma=False,
    )
```
